32 devices in a mesh: groups: 2 (over y), ulysses: 4 (over z), blk: 2 (over x), handoff: 2 (over core).
Axes of the slice: x: 2, y: 2, z: 4, core: 2. Of those that a mesh axis runs over, the one named last changes fastest.
Arguments:
- queries: bfloat16 [4, 512, 4096], P(('groups', 'handoff'), ('blk', 'ulysses')), parts along dimension 0, may hold values from -24 to 24
- keys: bfloat16 [4, 512, 2048], P(('groups', 'handoff'), ('blk', 'ulysses')), parts along dimension 0, may hold values from -7.5 to 7.5
- values: bfloat16 [4, 512, 2048], P(('groups', 'handoff'), ('blk', 'ulysses')), parts along dimension 0, may hold values from -6 to 6
- request_pages: int32 [4, 4], P('groups'), parts along dimension 0, may hold values from 1 to 4, 8 in all within a row
- page_table: int32 [4, 8], P('groups'), parts along dimension 0, may hold values from 0 to 15, as said below
Outputs:
- attended: bfloat16 [4, 512, 4096], P(('groups', 'handoff'), ('blk', 'ulysses')), parts along dimension 0
- cache_keys: bfloat16 [32, 16, 64, 128], P(('groups', 'blk', 'handoff'), 'ulysses'), parts along dimension 0
- cache_values: bfloat16 [32, 16, 64, 128], P(('groups', 'blk', 'handoff'), 'ulysses'), parts along dimension 0
The draws below stay inside these ranges and needn't reach their ends.
There are 2 independent parts, one for each index of `groups`. The reference program is written for one: setup_inputs(seed, part) draws one part's arguments, and reference() takes and returns one part's arrays. A program takes and returns all parts, laid end to end along the dimension named above; each array names one. Nothing has to cross between parts.
Inputs may be any that keep to these rules, and one draw needn't show every extreme that they name: `request_pages`: A pack's 4 requests fill its 8 pages; the longest holds exactly 4 of them. `page_table`: all rows together name every pool page once; the 4 pages of each aligned run of 4 pages of a pack's row go in equal numbers to each aligned run of 4 pool pages.
All inputs are finite; a program needn't handle non-finite values.
Results may differ from the reference program's by a relative error of at most 0.012.
Values may be sent and summed in bfloat16 or wider, within the bound.
A program may use at most 64 MiB of HBM per device.

```python
import math
import jax
import jax.numpy as jnp
import numpy as np
from jax import lax

QH = 32
KVH = 16
HD = 128
WINDOW = 4096
PAGE = 64
REQS = 4
SEQ = 512
PACKS = 2
PACK_PAGES = 8
SHARD_PAGES = 4
POOL = 16


def draw_queries(key, part):
    normal = jax.random.normal(jax.random.fold_in(key, 11), (PACKS, SEQ, QH * HD), jnp.float32)
    scaled = normal * 4.0
    return jnp.clip(scaled, -24.0, 24.0).astype(jnp.bfloat16)


def draw_page_table(key, part):
    slots_dev = SHARD_PAGES
    sources = POOL // SHARD_PAGES
    per_peer = slots_dev // sources
    lane_ids = jnp.arange(slots_dev, dtype=jnp.int32)[None, :]
    noise_one = jax.random.randint(jax.random.fold_in(key, 21), (sources, slots_dev), 0, 1 << 20) * slots_dev + lane_ids
    noise_two = jax.random.randint(jax.random.fold_in(key, 22), (sources, slots_dev), 0, 1 << 20) * slots_dev + lane_ids
    first_perm = jnp.argsort(noise_one, axis=1).astype(jnp.int32)
    second_perm = jnp.argsort(noise_two, axis=1).astype(jnp.int32)
    target = first_perm // per_peer
    within = first_perm % per_peer
    source_ids = jnp.arange(sources, dtype=jnp.int32)[:, None]
    slot_index = second_perm[target, source_ids * per_peer + within]
    pool_page = target * slots_dev + slot_index
    blk_lanes = sources // PACKS
    return jnp.transpose(pool_page.reshape(blk_lanes, PACKS, slots_dev), (1, 0, 2)).reshape(PACKS, PACK_PAGES).astype(jnp.int32)


def levels(stream_key, extent, shards, smallest, largest):
    def one(position, shards_of):
        heights = jax.random.uniform(jax.random.fold_in(jax.random.fold_in(stream_key, 6), position), (shards_of,), jnp.float32, smallest / len(shards), largest / len(shards))
        return jnp.repeat(jnp.exp(heights), extent[position] // shards_of).reshape((-1,) + (1,) * (len(extent) - position - 1))

    gain = one(*shards[0])
    for cut in shards[1:]:
        gain = gain * one(*cut)
    return gain


def split_up(count, total, most, skew):
    portions = [(1 << 20) // math.isqrt(standing ** skew) + 1 for standing in range(2, count + 1)]
    surplus, holding = total - most - (count - 1), [1] * (count - 1)
    while surplus > 0:
        movable = [i for i in range(count - 1) if holding[i] < most]
        pool, budget = sum([portions[i] for i in movable]), surplus
        for i in movable:
            extra = min(most - holding[i], max(1, budget * portions[i] // pool), surplus)
            holding[i] = holding[i] + extra
            surplus = surplus - extra
    return np.array([most] + holding)


def ragged(own_key, amount, total, limit, slope):
    if amount == 2:
        one = jax.random.randint(own_key, (), max(1, total - limit), min(limit, total - 1) + 1)
        return jnp.stack([one, total - one])
    lengths = jnp.asarray(split_up(amount, total, limit, slope), jnp.int32)
    twos = (amount - 1) // 2
    giver, receiver = lengths[1:1 + 2 * twos:2], lengths[2:2 + 2 * twos:2]
    slack = jnp.minimum(giver - 1, limit - receiver)
    moved = jax.random.randint(jax.random.fold_in(own_key, 1), (twos,), 0, 1 << 20) % (slack + 1)
    lengths = lengths.at[1:1 + 2 * twos:2].set(giver - moved).at[2:2 + 2 * twos:2].set(receiver + moved)
    return lengths[jax.random.permutation(jax.random.fold_in(own_key, 2), amount)]


def scatter_about(stream_key, dims, width, limit, pieces=(), kind=jnp.bfloat16):
    level = levels(stream_key, dims, pieces, -0.22, 0.18) if pieces else 1.0
    array = jax.random.normal(stream_key, dims, jnp.float32) * width * level
    return jnp.minimum(jnp.maximum(array, -limit), limit).astype(kind)


def setup_inputs(seed: int = 0, part: int = 0) -> dict:
    key_list = jax.random.split(jax.random.key(seed), 6)
    part_splits = jax.random.split(jax.random.fold_in(key_list[5], part), 6)
    queries = draw_queries(jax.random.fold_in(jax.random.fold_in(key_list[5], part), 71), part)
    keys = scatter_about(part_splits[1], (PACKS, SEQ, KVH * HD), 1.25, 7.5, ((0, 2), (1, 8)))
    values = scatter_about(part_splits[2], (PACKS, SEQ, KVH * HD), 1.0, 6.0, ((0, 2), (1, 8)))
    request_pages = jax.vmap(lambda own: ragged(own, REQS, PACK_PAGES, PACK_PAGES // 2, 1))(jax.random.split(part_splits[3], PACKS)).reshape((PACKS, REQS)).astype(jnp.int32)
    page_table = draw_page_table(jax.random.fold_in(jax.random.fold_in(key_list[5], part), 71), part)
    return dict(queries=queries, keys=keys, values=values, request_pages=request_pages, page_table=page_table)


QUERY_SCALE = 144.0 ** -0.5
SOFT_CAP = 50.0
ROPE_BASE = 10000.0


def request_marks(pages_row, positions):
    request_ends = jnp.cumsum(pages_row, dtype=jnp.int32) * PAGE
    request_starts = request_ends - pages_row * PAGE
    owner_index = jnp.sum((positions[:, None] >= request_ends[None, :]).astype(jnp.int32), axis=1)
    first_token = jnp.max(jnp.where(positions[:, None] >= request_starts[None, :], request_starts[None, :], 0), axis=1)
    return owner_index.astype(jnp.int32), (positions - first_token).astype(jnp.int32)


def rotate(head_rows, offsets):
    head_width = head_rows.shape[-1]
    half_width = head_width // 2
    frequency = ROPE_BASE ** (-(2.0 * jnp.arange(half_width, dtype=jnp.float32)) / head_width)
    angles = offsets.astype(jnp.float32)[:, None] * frequency[None, :]
    cosine = jnp.cos(angles)[:, None, :]
    sines = jnp.sin(angles)[:, None, :]
    as_float = head_rows.astype(jnp.float32)
    front_half = as_float[..., :half_width]
    back_half = as_float[..., half_width:]
    turned = jnp.concatenate([front_half * cosine - back_half * sines, back_half * cosine + front_half * sines], axis=-1)
    return turned.astype(jnp.bfloat16)


def reference(queries, keys, values, request_pages, page_table):
    group_size = QH // KVH
    block_rows = math.gcd(SEQ, 512)
    key_span = WINDOW + block_rows
    positions = jnp.arange(SEQ, dtype=jnp.int32)
    pad_positions = jnp.arange(SEQ + WINDOW, dtype=jnp.int32) - WINDOW
    outputs = []
    key_pages = []
    value_pages = []
    for pack_index in range(PACKS):
        owner_all, offsets = request_marks(request_pages[pack_index], positions)
        pad_owner, unused_offsets = request_marks(request_pages[pack_index], pad_positions)
        query_turned = rotate(queries[pack_index].reshape(SEQ, QH, HD), offsets)
        key_turned = rotate(keys[pack_index].reshape(SEQ, KVH, HD), offsets)
        value_heads = values[pack_index].reshape(SEQ, KVH, HD)
        pad_keys = jnp.concatenate([jnp.zeros((WINDOW, KVH, HD), jnp.bfloat16), key_turned], axis=0)
        pad_values = jnp.concatenate([jnp.zeros((WINDOW, KVH, HD), jnp.bfloat16), value_heads], axis=0)

        def attend(offset):
            query_block = lax.dynamic_slice_in_dim(query_turned, offset, block_rows, 0).astype(jnp.float32)
            query_block = query_block.reshape(block_rows, KVH, group_size, HD)
            key_block = lax.dynamic_slice_in_dim(pad_keys, offset, key_span, 0).astype(jnp.float32)
            value_block = lax.dynamic_slice_in_dim(pad_values, offset, key_span, 0).astype(jnp.float32)
            scores = jnp.einsum("qgrd,kgd->gqrk", query_block, key_block, precision=lax.Precision.HIGHEST) * QUERY_SCALE
            capped = SOFT_CAP * jnp.tanh(scores / SOFT_CAP)
            query_pos = lax.dynamic_slice_in_dim(positions, offset, block_rows)
            query_owner = lax.dynamic_slice_in_dim(owner_all, offset, block_rows)
            key_pos = lax.dynamic_slice_in_dim(pad_positions, offset, key_span)
            key_owner = lax.dynamic_slice_in_dim(pad_owner, offset, key_span)
            distance = query_pos[:, None] - key_pos[None, :]
            allowed = (query_owner[:, None] == key_owner[None, :]) & (distance >= 0) & (distance < WINDOW) & (key_pos[None, :] >= 0)
            weights = jnp.where(allowed[None, :, None, :], jnp.exp(capped), jnp.float32(0.0))
            totals = jnp.sum(weights, axis=-1)
            rounded = lax.optimization_barrier(weights.astype(jnp.bfloat16)).astype(jnp.float32)
            mixture = jnp.einsum("gqrk,kgd->qgrd", rounded, value_block, precision=lax.Precision.HIGHEST)
            return (mixture / jnp.transpose(totals, (1, 0, 2))[..., None]).astype(jnp.bfloat16)

        starts = jnp.arange(SEQ // block_rows, dtype=jnp.int32) * block_rows
        blocks = lax.map(attend, starts)
        outputs.append(blocks.reshape(SEQ, QH * HD))
        key_pages.append(key_turned.reshape(PACK_PAGES, PAGE, KVH, HD))
        value_pages.append(value_heads.reshape(PACK_PAGES, PAGE, KVH, HD))
    attended = jnp.stack(outputs)
    flat_keys = jnp.transpose(jnp.concatenate(key_pages, axis=0), (0, 2, 1, 3))
    flat_values = jnp.transpose(jnp.concatenate(value_pages, axis=0), (0, 2, 1, 3))
    pool_slots = page_table.reshape(-1).astype(jnp.int32)
    cache_keys = jnp.zeros_like(flat_keys).at[pool_slots].set(flat_keys)
    cache_values = jnp.zeros_like(flat_values).at[pool_slots].set(flat_values)
    return attended, cache_keys, cache_values
```

```python
import functools

import jax
import jax.numpy as jnp
import numpy as np
from jax import lax
from jax.experimental import pallas as pl
from jax.experimental.pallas import tpu as pltpu
from jax.sharding import PartitionSpec as P

QH = 32
KVH = 16
HD = 128
WINDOW = 4096
PAGE = 64

QUERY_SCALE = 144.0 ** (-0.5)
SOFT_CAP = 50.0
ROPE_BASE = 10000.0
MESH = pl.DeviceIdType.MESH


def turn(x, cosine, sine):
    wide = x.astype(jnp.float32)
    return (wide * cosine + pltpu.roll(wide, HD // 2, 1) * sine).astype(jnp.bfloat16)


def pick(index, choices):
    chosen = choices[0]
    for j in range(1, len(choices)):
        chosen = jnp.where(index == j, choices[j], chosen)
    return chosen


def kernel(
    sizes, q_ref, k_ref, v_ref, freq_ref, pages_ref, table_ref,
    out_ref, ck_ref, cv_ref,
    kraw, tab_k, tab_v, qbuf, obuf, cos_t, sin_t, out_k, out_v, got_k, got_v,
    in_send, in_recv, in_local, x_send, x_recv, c_send, c_recv, c_local, o_send, o_recv, o_local,
):
    ulysses, blks, cores, local, kvl, group, reach, reqs = sizes
    rows = ulysses * local
    slots = rows // PAGE
    sources = blks * cores
    back = min(-(-reach // rows), blks - 1)
    home = back * rows
    qw = group * HD
    me = lax.axis_index("ulysses")
    blk = lax.axis_index("blk")
    pack = lax.axis_index("handoff")
    mine = blk * cores + pack

    barrier = pltpu.get_barrier_semaphore()

    def u_peer(i):
        return lax.rem(me + i, ulysses)

    def s_peer(i):
        p = lax.rem(mine + i, sources)
        return p, {"blk": p // cores, "handoff": lax.rem(p, cores)}

    for i in range(1, ulysses):
        pl.semaphore_signal(barrier, inc=1, device_id={"ulysses": u_peer(i)}, device_id_type=MESH)
    for i in range(1, sources):
        pl.semaphore_signal(barrier, inc=1, device_id=s_peer(i)[1], device_id_type=MESH)

    for hop in range(1, back + 1):
        @pl.when(blk < hop)
        def _():
            part = pl.ds((back - hop) * rows, rows)
            tab_k[:, part, :] = jnp.zeros((kvl, rows, HD), jnp.bfloat16)
            tab_v[:, part, :] = jnp.zeros((kvl, rows, HD), jnp.bfloat16)

    pl.semaphore_wait(barrier, ulysses - 1 + sources - 1)

    def landing(what, h, whose):
        if what == 0:
            return kraw.at[h, pl.ds(whose * local, local), :]
        if what == 1:
            return tab_v.at[h, pl.ds(home + whose * local, local), :]
        return qbuf.at[h, pl.ds(whose * local, local), :]

    def leaving(what, h, whose):
        width = qw if what == 2 else HD
        ref = (k_ref, v_ref, q_ref)[what]
        return ref.at[:, pl.ds(pl.multiple_of((whose * kvl + h) * width, width), width)]

    def incoming(what, h, i):
        return pltpu.make_async_remote_copy(
            src_ref=leaving(what, h, u_peer(i)), dst_ref=landing(what, h, me),
            send_sem=in_send.at[what, h, i - 1], recv_sem=in_recv.at[what, h, i - 1],
            device_id={"ulysses": u_peer(i)}, device_id_type=MESH,
        )

    def own_in(what, h):
        return pltpu.make_async_copy(leaving(what, h, me), landing(what, h, me), in_local.at[what, h])

    order = [(w, h) for h in range(kvl) for w in (0, 1)] + [(2, h) for h in range(kvl)]
    for what, h in order:
        for i in range(1, ulysses):
            incoming(what, h, i).start()
        own_in(what, h).start()

    def arrive(what, h):
        own_in(what, h).wait()
        for i in range(1, ulysses):
            incoming(what, h, i).wait_recv()

    ends = []
    starts = []
    total = jnp.int32(0)
    for r in range(reqs):
        starts.append(total)
        total = total + pages_ref[pack, r] * PAGE
        ends.append(total)

    def first_token(pos):
        first = jnp.zeros_like(pos)
        for r in range(reqs):
            first = jnp.maximum(first, jnp.where(pos >= starts[r], starts[r], 0))
        return first

    pos_rows = blk * rows + lax.broadcasted_iota(jnp.int32, (rows, HD), 0)
    rel = (pos_rows - first_token(pos_rows)).astype(jnp.float32)
    angles = rel * freq_ref[...]
    lanes = lax.broadcasted_iota(jnp.int32, (rows, HD), 1)
    cos_t[...] = jnp.cos(angles)
    sine = jnp.sin(angles)
    sin_t[...] = jnp.where(lanes < HD // 2, -sine, sine)

    def onward(which, h, hop):
        tab = (tab_k, tab_v)[which]
        return pltpu.make_async_remote_copy(
            src_ref=tab.at[h, pl.ds(home, rows), :],
            dst_ref=tab.at[h, pl.ds((back - hop) * rows, rows), :],
            send_sem=x_send.at[which, h, hop - 1], recv_sem=x_recv.at[which, h, hop - 1],
            device_id={"blk": lax.rem(blk + hop, blks)}, device_id_type=MESH,
        )

    for h in range(kvl):
        arrive(0, h)
        tab_k[h, pl.ds(home, rows), :] = turn(kraw[h], cos_t[...], sin_t[...])
        arrive(1, h)
        for hop in range(1, back + 1):
            @pl.when(blk + hop < blks)
            def _():
                onward(0, h, hop).start()
                onward(1, h, hop).start()

    def page_for(owner):
        def step(j, found):
            page = table_ref[pack, blk * slots + j]
            return found + jnp.where(lax.div(page, jnp.int32(slots)) == owner, j, 0)
        return lax.fori_loop(0, slots, step, jnp.int32(0))

    def handed(which, i):
        src, dst = ((out_k, got_k), (out_v, got_v))[which]
        return pltpu.make_async_remote_copy(
            src_ref=src.at[i], dst_ref=dst.at[mine],
            send_sem=c_send.at[which, i - 1], recv_sem=c_recv.at[which, i - 1],
            device_id=s_peer(i)[1], device_id_type=MESH,
        )

    def own_page(which):
        src, dst = ((out_k, got_k), (out_v, got_v))[which]
        return pltpu.make_async_copy(src.at[0], dst.at[mine], c_local.at[which])

    for i in range(sources):
        chosen = page_for(s_peer(i)[0])
        for tab, out in ((tab_k, out_k), (tab_v, out_v)):
            out[i] = pick(chosen, [tab[:, home + j * PAGE:home + (j + 1) * PAGE, :] for j in range(slots)])
    for i in range(1, sources):
        handed(0, i).start()
        handed(1, i).start()
    own_page(0).start()
    own_page(1).start()

    block = min(rows, 128)
    lead = min(-(-reach // block) * block, home)
    span = lead + block
    chunk = span if span <= 512 else block
    factor = QUERY_SCALE / SOFT_CAP

    def attend(h, i):
        at = i * block
        if not isinstance(i, int):
            at = pl.multiple_of(at, block)
        here = pl.ds(at, block)
        cosine, sine_here = cos_t[here, :], sin_t[here, :]
        query = jnp.concatenate(
            [turn(qbuf[h, here, g * HD:(g + 1) * HD], cosine, sine_here) for g in range(group)], axis=0
        )
        pos = blk * rows + at + lax.broadcasted_iota(jnp.int32, (block, 1), 0)
        low = jnp.maximum(first_token(pos), pos - (WINDOW - 1))
        pos = jnp.concatenate([pos] * group, axis=0)
        low = jnp.concatenate([low] * group, axis=0)
        begin = home + at - lead

        def part(c):
            start = begin + c * chunk
            if not isinstance(start, int):
                start = pl.multiple_of(start, block)
            seen = pl.ds(start, chunk)
            scores = lax.dot_general(
                query, tab_k[h, seen, :], (((1,), (1,)), ((), ())), preferred_element_type=jnp.float32
            )
            weights = jnp.exp(SOFT_CAP * jnp.tanh(scores * factor))
            key_pos = (blk - back) * rows + start + lax.broadcasted_iota(jnp.int32, (1, chunk), 1)
            weights = jnp.where((key_pos <= pos) & (key_pos >= low), weights, 0.0)
            total = jnp.sum(weights, axis=1, keepdims=True)
            mixed = jnp.dot(
                weights.astype(jnp.bfloat16), tab_v[h, seen, :], preferred_element_type=jnp.float32
            )
            return mixed, total

        if span == chunk:
            mixed, total = part(0)
        else:
            def step(c, carry):
                mixed, total = part(c)
                return carry[0] + mixed, carry[1] + total
            mixed, total = lax.fori_loop(
                0, span // chunk, step,
                (jnp.zeros((group * block, HD), jnp.float32), jnp.zeros((group * block, 1), jnp.float32)),
            )
        result = (mixed / total).astype(jnp.bfloat16)
        for g in range(group):
            obuf[h, here, g * HD:(g + 1) * HD] = result[g * block:(g + 1) * block]

    def outgoing(h, i):
        return pltpu.make_async_remote_copy(
            src_ref=obuf.at[h, pl.ds(pl.multiple_of(u_peer(i) * local, local), local), :],
            dst_ref=out_ref.at[:, pl.ds(pl.multiple_of((me * kvl + h) * qw, qw), qw)],
            send_sem=o_send.at[h, i - 1], recv_sem=o_recv.at[h, i - 1],
            device_id={"ulysses": u_peer(i)}, device_id_type=MESH,
        )

    def own_out(h):
        return pltpu.make_async_copy(
            obuf.at[h, pl.ds(pl.multiple_of(me * local, local), local), :],
            out_ref.at[:, pl.ds(pl.multiple_of((me * kvl + h) * qw, qw), qw)],
            o_local.at[h],
        )

    for h in range(kvl):
        for hop in range(1, back + 1):
            @pl.when(blk >= hop)
            def _():
                onward(0, h, hop).wait_recv()
                onward(1, h, hop).wait_recv()
        arrive(2, h)
        if rows // block <= 4:
            for i in range(rows // block):
                attend(h, i)
        else:
            def each(i, carry):
                attend(h, i)
                return carry
            lax.fori_loop(0, rows // block, each, 0)
        for i in range(1, ulysses):
            outgoing(h, i).start()
        own_out(h).start()

    own_page(0).wait()
    own_page(1).wait()
    for i in range(1, sources):
        handed(0, i).wait_recv()
        handed(1, i).wait_recv()
    for j in range(slots):
        def step(n, found, j=j):
            s = n // slots
            page = table_ref[lax.rem(s, cores), (s // cores) * slots + lax.rem(n, slots)]
            return found + jnp.where(page == mine * slots + j, s, 0)
        source = lax.fori_loop(0, sources * slots, step, jnp.int32(0))
        ck_ref[j] = pick(source, [got_k[s] for s in range(sources)])
        cv_ref[j] = pick(source, [got_v[s] for s in range(sources)])

    for i in range(1, sources):
        handed(0, i).wait_send()
        handed(1, i).wait_send()
    for what, h in order:
        for i in range(1, ulysses):
            incoming(what, h, i).wait_send()
    for h in range(kvl):
        for hop in range(1, back + 1):
            @pl.when(blk + hop < blks)
            def _():
                onward(0, h, hop).wait_send()
                onward(1, h, hop).wait_send()
    for h in range(kvl):
        own_out(h).wait()
        for i in range(1, ulysses):
            outgoing(h, i).wait()


def paired(
    sizes, q_ref, k_ref, v_ref, freq_ref, pages_ref, table_ref,
    out_ref, ck_ref, cv_ref,
    qraw, kraw, qrot, krot, tab_k, tab_v, qbuf, obuf, out_k, out_v, got_k, got_v,
    load_sem, kv_send, kv_recv, v_local, q_send, q_recv, x_send, x_recv, c_send, c_recv, c_local, o_send, o_recv,
):
    ulysses, blks, cores, kvl, group, halo, reqs, per = sizes
    rows = ulysses * PAGE
    sources = blks * cores
    home = halo * PAGE
    picks = ulysses // 2
    steps = picks * kvl // per
    inner = kvl // per
    kw = per * HD
    qw = per * group * HD
    me = lax.axis_index("ulysses")
    blk = lax.axis_index("blk")
    pack = lax.axis_index("handoff")
    mine = blk * cores + pack
    side = lax.rem(me, 2)
    duo = lax.div(me, 2)
    mate = me + 1 - 2 * side

    loads = [
        pltpu.make_async_copy(k_ref, kraw, load_sem.at[0]),
        pltpu.make_async_copy(q_ref, qraw, load_sem.at[1]),
    ]
    for load in loads:
        load.start()

    barrier = pltpu.get_barrier_semaphore()

    def u_peer(i):
        return lax.rem(me + i, ulysses)

    def u_source(i):
        return lax.rem(me + ulysses - i, ulysses)

    def s_peer(i):
        p = lax.rem(mine + i, sources)
        return p, {"blk": p // cores, "handoff": lax.rem(p, cores)}

    for i in range(1, ulysses):
        pl.semaphore_signal(barrier, inc=1, device_id={"ulysses": u_peer(i)}, device_id_type=MESH)
    for i in range(1, sources):
        pl.semaphore_signal(barrier, inc=1, device_id=s_peer(i)[1], device_id_type=MESH)

    def columns(whose, t, width):
        chosen = lax.rem(whose + 2 * (t // inner), ulysses)
        return pl.ds(pl.multiple_of((chosen * inner + t % inner) * width, width), width)

    def page_rows(page):
        return pl.ds(pl.multiple_of(home + page * PAGE, PAGE), PAGE)

    own_rows = pl.ds(pl.multiple_of(side * PAGE, PAGE), PAGE)
    mate_rows = pl.ds(pl.multiple_of((1 - side) * PAGE, PAGE), PAGE)

    def own_values(t):
        return pltpu.make_async_copy(
            v_ref.at[:, columns(me, t, kw)], tab_v.at[page_rows(me), t * kw:(t + 1) * kw], v_local.at[t]
        )

    for t in range(steps):
        own_values(t).start()

    @pl.when(blk == 0)
    def _():
        tab_k[0:home, :] = jnp.zeros((home, steps * kw), jnp.bfloat16)
        tab_v[0:home, :] = jnp.zeros((home, steps * kw), jnp.bfloat16)

    starts = []
    total = jnp.int32(0)
    for r in range(reqs):
        starts.append(total)
        total = total + pages_ref[pack, r] * PAGE

    def first_token(pos):
        first = jnp.zeros_like(pos)
        for r in range(reqs):
            first = jnp.maximum(first, jnp.where(pos >= starts[r], starts[r], 0))
        return first

    pos = blk * rows + me * PAGE + lax.broadcasted_iota(jnp.int32, (PAGE, HD), 0)
    angles = (pos - first_token(pos)).astype(jnp.float32) * freq_ref[...]
    lanes = lax.broadcasted_iota(jnp.int32, (PAGE, HD), 1)
    cosine = jnp.cos(angles)
    sine = jnp.sin(angles)
    sine = jnp.where(lanes < HD // 2, -sine, sine)

    loads[0].wait()
    for h in range(KVH):
        at = slice(h * HD, (h + 1) * HD)
        krot[:, at] = turn(kraw[:, at], cosine, sine)
    loads[1].wait()
    for h in range(KVH * group):
        at = slice(h * HD, (h + 1) * HD)
        qrot[:, at] = turn(qraw[:, at], cosine, sine)

    pl.semaphore_wait(barrier, ulysses - 1 + sources - 1)

    def needed(page, reader, t):
        if t < inner:
            return None
        lower = page <= 2 * lax.div(reader, 2) + 1
        return lower | (blk + 1 < blks)

    def guarded(condition, action):
        if condition is None:
            action()
        else:
            pl.when(condition)(action)

    def spread(which, t, i):
        src = (krot, v_ref)[which]
        tab = (tab_k, tab_v)[which]
        return pltpu.make_async_remote_copy(
            src_ref=src.at[:, columns(u_peer(i), t, kw)],
            dst_ref=tab.at[page_rows(me), t * kw:(t + 1) * kw],
            send_sem=kv_send.at[which, t, i - 1], recv_sem=kv_recv.at[which, t, i - 1],
            device_id={"ulysses": u_peer(i)}, device_id_type=MESH,
        )

    def asked(t):
        return pltpu.make_async_remote_copy(
            src_ref=qrot.at[:, columns(mate, t, qw)],
            dst_ref=qbuf.at[own_rows, t * qw:(t + 1) * qw],
            send_sem=q_send.at[t], recv_sem=q_recv.at[t],
            device_id={"ulysses": mate}, device_id_type=MESH,
        )

    for t in range(steps):
        for i in range(1, ulysses):
            def go(i=i, t=t):
                spread(0, t, i).start()
                spread(1, t, i).start()
            guarded(needed(me, u_peer(i), t), go)
        asked(t).start()

    for t in range(steps):
        tab_k[page_rows(me), t * kw:(t + 1) * kw] = krot[:, columns(me, t, kw)]
        qbuf[own_rows, t * qw:(t + 1) * qw] = qrot[:, columns(me, t, qw)]

    def onward(which, t, low):
        tab = (tab_k, tab_v)[which]
        count = (halo - low) * PAGE
        return pltpu.make_async_remote_copy(
            src_ref=tab.at[home + rows - count:home + rows, t * kw:(t + 1) * kw],
            dst_ref=tab.at[low * PAGE:halo * PAGE, t * kw:(t + 1) * kw],
            send_sem=x_send.at[which, t], recv_sem=x_recv.at[which, t],
            device_id={"blk": lax.rem(blk + 1, blks)}, device_id_type=MESH,
        )

    def each_halo(condition, action):
        for d in range(ulysses // 2):
            if 2 * d < halo:
                pl.when(condition & (duo == d))(functools.partial(action, 2 * d))

    def page_for(owner):
        def step(j, found):
            page = table_ref[pack, blk * ulysses + j]
            return found + jnp.where(lax.div(page, jnp.int32(ulysses)) == owner, j, 0)
        return lax.fori_loop(0, ulysses, step, jnp.int32(0))

    def handed(which, i):
        src, dst = ((out_k, got_k), (out_v, got_v))[which]
        return pltpu.make_async_remote_copy(
            src_ref=src.at[i], dst_ref=dst.at[mine],
            send_sem=c_send.at[which, i - 1], recv_sem=c_recv.at[which, i - 1],
            device_id=s_peer(i)[1], device_id_type=MESH,
        )

    def own_page(which):
        src, dst = ((out_k, got_k), (out_v, got_v))[which]
        return pltpu.make_async_copy(src.at[0], dst.at[mine], c_local.at[which])

    def hand_over():
        for i in range(sources):
            chosen = page_for(s_peer(i)[0])
            for tab, out in ((tab_k, out_k), (tab_v, out_v)):
                for h in range(kvl):
                    out[i, h] = pick(chosen, [
                        tab[home + j * PAGE:home + (j + 1) * PAGE, h * HD:(h + 1) * HD] for j in range(ulysses)
                    ])
        for i in range(1, sources):
            handed(0, i).start()
            handed(1, i).start()
        own_page(0).start()
        own_page(1).start()

    block = 2 * PAGE
    span = home + block
    factor = QUERY_SCALE / SOFT_CAP
    begin = pl.multiple_of(duo * block, block)
    seen = pl.ds(begin, span)
    q_pos = blk * rows + duo * block + lax.broadcasted_iota(jnp.int32, (block, 1), 0)
    q_low = jnp.maximum(first_token(q_pos), q_pos - (WINDOW - 1))
    key_pos = blk * rows - home + begin + lax.broadcasted_iota(jnp.int32, (1, span), 1)
    allowed = (key_pos <= q_pos) & (key_pos >= q_low)
    allowed = jnp.concatenate([allowed] * group, axis=0)

    def attend(h):
        query = jnp.concatenate(
            [qbuf[:, (h * group + g) * HD:(h * group + g + 1) * HD] for g in range(group)], axis=0
        )
        scores = lax.dot_general(
            query, tab_k[seen, h * HD:(h + 1) * HD], (((1,), (1,)), ((), ())), preferred_element_type=jnp.float32
        )
        weights = jnp.exp(SOFT_CAP * jnp.tanh(scores * factor))
        weights = jnp.where(allowed, weights, 0.0)
        total = jnp.sum(weights, axis=1, keepdims=True)
        mixed = jnp.dot(
            weights.astype(jnp.bfloat16), tab_v[seen, h * HD:(h + 1) * HD], preferred_element_type=jnp.float32
        )
        result = (mixed / total).astype(jnp.bfloat16)
        for g in range(group):
            obuf[:, (h * group + g) * HD:(h * group + g + 1) * HD] = result[g * block:(g + 1) * block]

    def outgoing(t):
        return pltpu.make_async_remote_copy(
            src_ref=obuf.at[mate_rows, t * qw:(t + 1) * qw],
            dst_ref=out_ref.at[:, columns(me, t, qw)],
            send_sem=o_send.at[t], recv_sem=o_recv.at[t],
            device_id={"ulysses": mate}, device_id_type=MESH,
        )

    for t in range(steps):
        own_values(t).wait()
        for i in range(1, ulysses):
            def landed(i=i, t=t):
                spread(0, t, i).wait_recv()
                spread(1, t, i).wait_recv()
            guarded(needed(u_source(i), me, t), landed)

        def send_on(low, t=t):
            onward(0, t, low).start()
            onward(1, t, low).start()

        def receive(low, t=t):
            onward(0, t, low).wait_recv()
            onward(1, t, low).wait_recv()

        each_halo(blk + 1 < blks, send_on)
        if t == inner - 1:
            hand_over()
        each_halo(blk > 0, receive)
        asked(t).wait_recv()
        for h in range(t * per, (t + 1) * per):
            attend(h)
        outgoing(t).start()
        out_ref[:, columns(me, t, qw)] = obuf[own_rows, t * qw:(t + 1) * qw]

    own_page(0).wait()
    own_page(1).wait()
    for i in range(1, sources):
        handed(0, i).wait_recv()
        handed(1, i).wait_recv()
    for j in range(ulysses):
        def step(n, found, j=j):
            s = n // ulysses
            page = table_ref[lax.rem(s, cores), (s // cores) * ulysses + lax.rem(n, ulysses)]
            return found + jnp.where(page == mine * ulysses + j, s, 0)
        source = lax.fori_loop(0, sources * ulysses, step, jnp.int32(0))
        ck_ref[j] = pick(source, [got_k[s] for s in range(sources)])
        cv_ref[j] = pick(source, [got_v[s] for s in range(sources)])

    for i in range(1, sources):
        handed(0, i).wait_send()
        handed(1, i).wait_send()
    for t in range(steps):
        for i in range(1, ulysses):
            def sent(i=i, t=t):
                spread(0, t, i).wait_send()
                spread(1, t, i).wait_send()
            guarded(needed(me, u_peer(i), t), sent)
        asked(t).wait_send()

        def passed(low, t=t):
            onward(0, t, low).wait_send()
            onward(1, t, low).wait_send()

        each_halo(blk + 1 < blks, passed)
        outgoing(t).wait()


def place(*refs):
    count = (len(refs) - 1) // 2
    sem = refs[-1]
    copies = [pltpu.make_async_copy(refs[i], refs[count + i], sem.at[i]) for i in range(count)]
    for copy in copies:
        copy.start()
    for copy in copies:
        copy.wait()


def body(queries, keys, values, request_pages, page_table):
    local = queries.shape[1]
    ulysses = lax.axis_size("ulysses")
    blks = lax.axis_size("blk")
    cores = lax.axis_size("handoff")
    kvl = KVH // ulysses
    group = QH // KVH
    rows = local * ulysses
    slots = rows // PAGE
    sources = blks * cores
    assert slots == sources
    reach = min(WINDOW, page_table.shape[1] // 2 * PAGE)
    back = min(-(-reach // rows), blks - 1)
    reqs = request_pages.shape[1]
    half = np.arange(HD // 2, dtype=np.float64)
    freq = (ROPE_BASE ** (-2.0 * half / HD)).astype(np.float32)
    freq = jnp.asarray(np.concatenate([freq, freq])[None, :])
    sizes = (ulysses, blks, cores, local, kvl, group, reach, reqs)
    qw = group * HD
    halo = reach // PAGE - 1
    per = min(2, kvl)
    bf = jnp.bfloat16
    dma = pltpu.SemaphoreType.DMA
    hops = max(back, 1)
    anywhere = pl.BlockSpec(memory_space=pl.ANY)
    vmem = pl.BlockSpec(memory_space=pltpu.VMEM)
    smem = pl.BlockSpec(memory_space=pltpu.SMEM)
    narrow = local == PAGE and ulysses % 2 == 0 and 0 < halo <= ulysses and kvl % per == 0 and blks > 1
    if narrow:
        held = ulysses // 2 * kvl
        steps = held // per
        run = functools.partial(paired, (ulysses, blks, cores, kvl, group, halo, reqs, per))
        table = pltpu.VMEM((halo * PAGE + rows, held * HD), bf)
        handing = pltpu.VMEM((sources, kvl, PAGE, HD), bf)
        scratch = [
            pltpu.VMEM((PAGE, QH * HD), bf),
            pltpu.VMEM((PAGE, KVH * HD), bf),
            pltpu.VMEM((PAGE, QH * HD), bf),
            pltpu.VMEM((PAGE, KVH * HD), bf),
            table, table,
            pltpu.VMEM((2 * PAGE, held * qw), bf),
            pltpu.VMEM((2 * PAGE, held * qw), bf),
            handing, handing, handing, handing,
            dma((2,)),
            dma((2, steps, ulysses - 1)),
            dma((2, steps, ulysses - 1)),
            dma((steps,)),
            dma((steps,)),
            dma((steps,)),
            dma((2, steps)),
            dma((2, steps)),
            dma((2, sources - 1)),
            dma((2, sources - 1)),
            dma((2,)),
            dma((steps,)),
            dma((steps,)),
        ]
    else:
        run = functools.partial(kernel, sizes)
        scratch = [
            pltpu.VMEM((kvl, rows, HD), bf),
            pltpu.VMEM((kvl, (back + 1) * rows, HD), bf),
            pltpu.VMEM((kvl, (back + 1) * rows, HD), bf),
            pltpu.VMEM((kvl, rows, qw), bf),
            pltpu.VMEM((kvl, rows, qw), bf),
            pltpu.VMEM((rows, HD), jnp.float32),
            pltpu.VMEM((rows, HD), jnp.float32),
            pltpu.VMEM((sources, kvl, PAGE, HD), bf),
            pltpu.VMEM((sources, kvl, PAGE, HD), bf),
            pltpu.VMEM((sources, kvl, PAGE, HD), bf),
            pltpu.VMEM((sources, kvl, PAGE, HD), bf),
            dma((3, kvl, ulysses - 1)),
            dma((3, kvl, ulysses - 1)),
            dma((3, kvl)),
            dma((2, kvl, hops)),
            dma((2, kvl, hops)),
            dma((2, sources - 1)),
            dma((2, sources - 1)),
            dma((2,)),
            dma((kvl, ulysses - 1)),
            dma((kvl, ulysses - 1)),
            dma((kvl,)),
        ]
    results = pl.pallas_call(
        run,
        out_shape=(
            pltpu.VMEM((local, QH * HD), bf),
            pltpu.VMEM((slots, kvl, PAGE, HD), bf),
            pltpu.VMEM((slots, kvl, PAGE, HD), bf),
        ),
        in_specs=[anywhere, anywhere, anywhere, vmem, smem, smem],
        out_specs=(vmem, vmem, vmem),
        scratch_shapes=scratch,
        compiler_params=pltpu.CompilerParams(collective_id=0, has_side_effects=True),
    )(queries[0], keys[0], values[0], freq, request_pages, page_table)
    results = [pltpu.with_memory_space_constraint(x, pltpu.VMEM) for x in results]
    attended, cache_keys, cache_values = pl.pallas_call(
        place,
        out_shape=tuple(jax.ShapeDtypeStruct(x.shape, x.dtype) for x in results),
        in_specs=[anywhere] * len(results),
        out_specs=(anywhere,) * len(results),
        scratch_shapes=[dma((len(results),))],
        compiler_params=pltpu.CompilerParams(vmem_limit_bytes=1 << 20),
    )(*results)
    return (attended[None], cache_keys, cache_values)


def solution(mesh):
    in_specs = (
        P(("groups", "handoff"), ("blk", "ulysses"), None),
        P(("groups", "handoff"), ("blk", "ulysses"), None),
        P(("groups", "handoff"), ("blk", "ulysses"), None),
        P("groups", None),
        P("groups", None),
    )
    out_specs = (
        P(("groups", "handoff"), ("blk", "ulysses"), None),
        P(("groups", "blk", "handoff"), "ulysses", None, None),
        P(("groups", "blk", "handoff"), "ulysses", None, None),
    )
    return jax.shard_map(body, mesh=mesh, in_specs=in_specs, out_specs=out_specs, check_vma=False)
```

```python
import functools

import jax
import jax.numpy as jnp
import numpy as np
from jax import lax
from jax.experimental import pallas as pl
from jax.experimental.pallas import tpu as pltpu
from jax.sharding import PartitionSpec as P

QH = 32
KVH = 16
HD = 128
WINDOW = 4096
PAGE = 64

QUERY_SCALE = 144.0 ** (-0.5)
SOFT_CAP = 50.0
ROPE_BASE = 10000.0
MESH = pl.DeviceIdType.MESH


def turn(x, cosine, sine):
    wide = x.astype(jnp.float32)
    return (wide * cosine + pltpu.roll(wide, HD // 2, 1) * sine).astype(jnp.bfloat16)


def pick(index, choices):
    chosen = choices[0]
    for j in range(1, len(choices)):
        chosen = jnp.where(index == j, choices[j], chosen)
    return chosen


def kernel(
    sizes, q_ref, k_ref, v_ref, freq_ref, pages_ref, table_ref,
    out_ref, ck_ref, cv_ref,
    kraw, tab_k, tab_v, qbuf, obuf, cos_t, sin_t, out_k, out_v, got_k, got_v,
    in_send, in_recv, in_local, x_send, x_recv, c_send, c_recv, c_local, o_send, o_recv, o_local,
):
    ulysses, blks, cores, local, kvl, group, reach, reqs = sizes
    rows = ulysses * local
    slots = rows // PAGE
    sources = blks * cores
    back = min(-(-reach // rows), blks - 1)
    home = back * rows
    qw = group * HD
    me = lax.axis_index("ulysses")
    blk = lax.axis_index("blk")
    pack = lax.axis_index("handoff")
    mine = blk * cores + pack

    barrier = pltpu.get_barrier_semaphore()

    def u_peer(i):
        return lax.rem(me + i, ulysses)

    def s_peer(i):
        p = lax.rem(mine + i, sources)
        return p, {"blk": p // cores, "handoff": lax.rem(p, cores)}

    for i in range(1, ulysses):
        pl.semaphore_signal(barrier, inc=1, device_id={"ulysses": u_peer(i)}, device_id_type=MESH)
    for i in range(1, sources):
        pl.semaphore_signal(barrier, inc=1, device_id=s_peer(i)[1], device_id_type=MESH)

    for hop in range(1, back + 1):
        @pl.when(blk < hop)
        def _():
            part = pl.ds((back - hop) * rows, rows)
            tab_k[:, part, :] = jnp.zeros((kvl, rows, HD), jnp.bfloat16)
            tab_v[:, part, :] = jnp.zeros((kvl, rows, HD), jnp.bfloat16)

    pl.semaphore_wait(barrier, ulysses - 1 + sources - 1)

    def landing(what, h, whose):
        if what == 0:
            return kraw.at[h, pl.ds(whose * local, local), :]
        if what == 1:
            return tab_v.at[h, pl.ds(home + whose * local, local), :]
        return qbuf.at[h, pl.ds(whose * local, local), :]

    def leaving(what, h, whose):
        width = qw if what == 2 else HD
        ref = (k_ref, v_ref, q_ref)[what]
        return ref.at[:, pl.ds(pl.multiple_of((whose * kvl + h) * width, width), width)]

    def incoming(what, h, i):
        return pltpu.make_async_remote_copy(
            src_ref=leaving(what, h, u_peer(i)), dst_ref=landing(what, h, me),
            send_sem=in_send.at[what, h, i - 1], recv_sem=in_recv.at[what, h, i - 1],
            device_id={"ulysses": u_peer(i)}, device_id_type=MESH,
        )

    def own_in(what, h):
        return pltpu.make_async_copy(leaving(what, h, me), landing(what, h, me), in_local.at[what, h])

    order = [(w, h) for h in range(kvl) for w in (0, 1)] + [(2, h) for h in range(kvl)]
    for what, h in order:
        for i in range(1, ulysses):
            incoming(what, h, i).start()
        own_in(what, h).start()

    def arrive(what, h):
        own_in(what, h).wait()
        for i in range(1, ulysses):
            incoming(what, h, i).wait_recv()

    ends = []
    starts = []
    total = jnp.int32(0)
    for r in range(reqs):
        starts.append(total)
        total = total + pages_ref[pack, r] * PAGE
        ends.append(total)

    def first_token(pos):
        first = jnp.zeros_like(pos)
        for r in range(reqs):
            first = jnp.maximum(first, jnp.where(pos >= starts[r], starts[r], 0))
        return first

    pos_rows = blk * rows + lax.broadcasted_iota(jnp.int32, (rows, HD), 0)
    rel = (pos_rows - first_token(pos_rows)).astype(jnp.float32)
    angles = rel * freq_ref[...]
    lanes = lax.broadcasted_iota(jnp.int32, (rows, HD), 1)
    cos_t[...] = jnp.cos(angles)
    sine = jnp.sin(angles)
    sin_t[...] = jnp.where(lanes < HD // 2, -sine, sine)

    def onward(which, h, hop):
        tab = (tab_k, tab_v)[which]
        return pltpu.make_async_remote_copy(
            src_ref=tab.at[h, pl.ds(home, rows), :],
            dst_ref=tab.at[h, pl.ds((back - hop) * rows, rows), :],
            send_sem=x_send.at[which, h, hop - 1], recv_sem=x_recv.at[which, h, hop - 1],
            device_id={"blk": lax.rem(blk + hop, blks)}, device_id_type=MESH,
        )

    for h in range(kvl):
        arrive(0, h)
        tab_k[h, pl.ds(home, rows), :] = turn(kraw[h], cos_t[...], sin_t[...])
        arrive(1, h)
        for hop in range(1, back + 1):
            @pl.when(blk + hop < blks)
            def _():
                onward(0, h, hop).start()
                onward(1, h, hop).start()

    def page_for(owner):
        def step(j, found):
            page = table_ref[pack, blk * slots + j]
            return found + jnp.where(lax.div(page, jnp.int32(slots)) == owner, j, 0)
        return lax.fori_loop(0, slots, step, jnp.int32(0))

    def handed(which, i):
        src, dst = ((out_k, got_k), (out_v, got_v))[which]
        return pltpu.make_async_remote_copy(
            src_ref=src.at[i], dst_ref=dst.at[mine],
            send_sem=c_send.at[which, i - 1], recv_sem=c_recv.at[which, i - 1],
            device_id=s_peer(i)[1], device_id_type=MESH,
        )

    def own_page(which):
        src, dst = ((out_k, got_k), (out_v, got_v))[which]
        return pltpu.make_async_copy(src.at[0], dst.at[mine], c_local.at[which])

    for i in range(sources):
        chosen = page_for(s_peer(i)[0])
        for tab, out in ((tab_k, out_k), (tab_v, out_v)):
            out[i] = pick(chosen, [tab[:, home + j * PAGE:home + (j + 1) * PAGE, :] for j in range(slots)])
    for i in range(1, sources):
        handed(0, i).start()
        handed(1, i).start()
    own_page(0).start()
    own_page(1).start()

    block = min(rows, 128)
    lead = min(-(-reach // block) * block, home)
    span = lead + block
    chunk = span if span <= 512 else block
    factor = QUERY_SCALE / SOFT_CAP

    def attend(h, i):
        at = i * block
        if not isinstance(i, int):
            at = pl.multiple_of(at, block)
        here = pl.ds(at, block)
        cosine, sine_here = cos_t[here, :], sin_t[here, :]
        query = jnp.concatenate(
            [turn(qbuf[h, here, g * HD:(g + 1) * HD], cosine, sine_here) for g in range(group)], axis=0
        )
        pos = blk * rows + at + lax.broadcasted_iota(jnp.int32, (block, 1), 0)
        low = jnp.maximum(first_token(pos), pos - (WINDOW - 1))
        pos = jnp.concatenate([pos] * group, axis=0)
        low = jnp.concatenate([low] * group, axis=0)
        begin = home + at - lead

        def part(c):
            start = begin + c * chunk
            if not isinstance(start, int):
                start = pl.multiple_of(start, block)
            seen = pl.ds(start, chunk)
            scores = lax.dot_general(
                query, tab_k[h, seen, :], (((1,), (1,)), ((), ())), preferred_element_type=jnp.float32
            )
            weights = jnp.exp(SOFT_CAP * jnp.tanh(scores * factor))
            key_pos = (blk - back) * rows + start + lax.broadcasted_iota(jnp.int32, (1, chunk), 1)
            weights = jnp.where((key_pos <= pos) & (key_pos >= low), weights, 0.0)
            total = jnp.sum(weights, axis=1, keepdims=True)
            mixed = jnp.dot(
                weights.astype(jnp.bfloat16), tab_v[h, seen, :], preferred_element_type=jnp.float32
            )
            return mixed, total

        if span == chunk:
            mixed, total = part(0)
        else:
            def step(c, carry):
                mixed, total = part(c)
                return carry[0] + mixed, carry[1] + total
            mixed, total = lax.fori_loop(
                0, span // chunk, step,
                (jnp.zeros((group * block, HD), jnp.float32), jnp.zeros((group * block, 1), jnp.float32)),
            )
        result = (mixed / total).astype(jnp.bfloat16)
        for g in range(group):
            obuf[h, here, g * HD:(g + 1) * HD] = result[g * block:(g + 1) * block]

    def outgoing(h, i):
        return pltpu.make_async_remote_copy(
            src_ref=obuf.at[h, pl.ds(pl.multiple_of(u_peer(i) * local, local), local), :],
            dst_ref=out_ref.at[:, pl.ds(pl.multiple_of((me * kvl + h) * qw, qw), qw)],
            send_sem=o_send.at[h, i - 1], recv_sem=o_recv.at[h, i - 1],
            device_id={"ulysses": u_peer(i)}, device_id_type=MESH,
        )

    def own_out(h):
        return pltpu.make_async_copy(
            obuf.at[h, pl.ds(pl.multiple_of(me * local, local), local), :],
            out_ref.at[:, pl.ds(pl.multiple_of((me * kvl + h) * qw, qw), qw)],
            o_local.at[h],
        )

    for h in range(kvl):
        for hop in range(1, back + 1):
            @pl.when(blk >= hop)
            def _():
                onward(0, h, hop).wait_recv()
                onward(1, h, hop).wait_recv()
        arrive(2, h)
        if rows // block <= 4:
            for i in range(rows // block):
                attend(h, i)
        else:
            def each(i, carry):
                attend(h, i)
                return carry
            lax.fori_loop(0, rows // block, each, 0)
        for i in range(1, ulysses):
            outgoing(h, i).start()
        own_out(h).start()

    own_page(0).wait()
    own_page(1).wait()
    for i in range(1, sources):
        handed(0, i).wait_recv()
        handed(1, i).wait_recv()
    for j in range(slots):
        def step(n, found, j=j):
            s = n // slots
            page = table_ref[lax.rem(s, cores), (s // cores) * slots + lax.rem(n, slots)]
            return found + jnp.where(page == mine * slots + j, s, 0)
        source = lax.fori_loop(0, sources * slots, step, jnp.int32(0))
        ck_ref[j] = pick(source, [got_k[s] for s in range(sources)])
        cv_ref[j] = pick(source, [got_v[s] for s in range(sources)])

    for i in range(1, sources):
        handed(0, i).wait_send()
        handed(1, i).wait_send()
    for what, h in order:
        for i in range(1, ulysses):
            incoming(what, h, i).wait_send()
    for h in range(kvl):
        for hop in range(1, back + 1):
            @pl.when(blk + hop < blks)
            def _():
                onward(0, h, hop).wait_send()
                onward(1, h, hop).wait_send()
    for h in range(kvl):
        own_out(h).wait()
        for i in range(1, ulysses):
            outgoing(h, i).wait()


def paired(
    sizes, q_ref, k_ref, v_ref, freq_ref, pages_ref, table_ref,
    out_ref, ck_ref, cv_ref,
    qraw, kraw, qrot, krot, tab_k, tab_v, qbuf, obuf, out_k, out_v, got_k, got_v,
    load_sem, kv_send, kv_recv, v_local, q_send, q_recv, x_send, x_recv, c_send, c_recv, c_local, o_send, o_recv,
):
    ulysses, blks, cores, kvl, group, halo, reqs, per = sizes
    rows = ulysses * PAGE
    sources = blks * cores
    home = halo * PAGE
    picks = ulysses // 2
    steps = picks * kvl // per
    inner = kvl // per
    kw = per * HD
    qw = per * group * HD
    me = lax.axis_index("ulysses")
    blk = lax.axis_index("blk")
    pack = lax.axis_index("handoff")
    mine = blk * cores + pack
    side = lax.rem(me, 2)
    duo = lax.div(me, 2)
    mate = me + 1 - 2 * side

    loads = [
        pltpu.make_async_copy(k_ref, kraw, load_sem.at[0]),
        pltpu.make_async_copy(q_ref, qraw, load_sem.at[1]),
    ]
    for load in loads:
        load.start()

    barrier = pltpu.get_barrier_semaphore()

    def u_peer(i):
        return lax.rem(me + i, ulysses)

    def u_source(i):
        return lax.rem(me + ulysses - i, ulysses)

    def s_peer(i):
        p = lax.rem(mine + i, sources)
        return p, {"blk": p // cores, "handoff": lax.rem(p, cores)}

    for i in range(1, ulysses):
        pl.semaphore_signal(barrier, inc=1, device_id={"ulysses": u_peer(i)}, device_id_type=MESH)
    for i in range(1, sources):
        pl.semaphore_signal(barrier, inc=1, device_id=s_peer(i)[1], device_id_type=MESH)

    def columns(whose, t, width):
        chosen = lax.rem(whose + 2 * (t // inner), ulysses)
        return pl.ds(pl.multiple_of((chosen * inner + t % inner) * width, width), width)

    def page_rows(page):
        return pl.ds(pl.multiple_of(home + page * PAGE, PAGE), PAGE)

    own_rows = pl.ds(pl.multiple_of(side * PAGE, PAGE), PAGE)
    mate_rows = pl.ds(pl.multiple_of((1 - side) * PAGE, PAGE), PAGE)

    def own_values(t):
        return pltpu.make_async_copy(
            v_ref.at[:, columns(me, t, kw)], tab_v.at[page_rows(me), t * kw:(t + 1) * kw], v_local.at[t]
        )

    for t in range(steps):
        own_values(t).start()

    @pl.when(blk == 0)
    def _():
        tab_k[0:home, :] = jnp.zeros((home, steps * kw), jnp.bfloat16)
        tab_v[0:home, :] = jnp.zeros((home, steps * kw), jnp.bfloat16)

    starts = []
    total = jnp.int32(0)
    for r in range(reqs):
        starts.append(total)
        total = total + pages_ref[pack, r] * PAGE

    def first_token(pos):
        first = jnp.zeros_like(pos)
        for r in range(reqs):
            first = jnp.maximum(first, jnp.where(pos >= starts[r], starts[r], 0))
        return first

    pos = blk * rows + me * PAGE + lax.broadcasted_iota(jnp.int32, (PAGE, HD), 0)
    angles = (pos - first_token(pos)).astype(jnp.float32) * freq_ref[...]
    lanes = lax.broadcasted_iota(jnp.int32, (PAGE, HD), 1)
    cosine = jnp.cos(angles)
    sine = jnp.sin(angles)
    sine = jnp.where(lanes < HD // 2, -sine, sine)

    loads[0].wait()
    for h in range(KVH):
        at = slice(h * HD, (h + 1) * HD)
        krot[:, at] = turn(kraw[:, at], cosine, sine)
    loads[1].wait()
    for h in range(KVH * group):
        at = slice(h * HD, (h + 1) * HD)
        qrot[:, at] = turn(qraw[:, at], cosine, sine)

    pl.semaphore_wait(barrier, ulysses - 1 + sources - 1)

    def needed(page, reader, t):
        if t < inner:
            return None
        lower = page <= 2 * lax.div(reader, 2) + 1
        return lower | (blk + 1 < blks)

    def guarded(condition, action):
        if condition is None:
            action()
        else:
            pl.when(condition)(action)

    def spread(which, t, i):
        src = (krot, v_ref)[which]
        tab = (tab_k, tab_v)[which]
        return pltpu.make_async_remote_copy(
            src_ref=src.at[:, columns(u_peer(i), t, kw)],
            dst_ref=tab.at[page_rows(me), t * kw:(t + 1) * kw],
            send_sem=kv_send.at[which, t, i - 1], recv_sem=kv_recv.at[which, t, i - 1],
            device_id={"ulysses": u_peer(i)}, device_id_type=MESH,
        )

    def asked(t):
        return pltpu.make_async_remote_copy(
            src_ref=qrot.at[:, columns(mate, t, qw)],
            dst_ref=qbuf.at[own_rows, t * qw:(t + 1) * qw],
            send_sem=q_send.at[t], recv_sem=q_recv.at[t],
            device_id={"ulysses": mate}, device_id_type=MESH,
        )

    for t in range(steps):
        for i in range(1, ulysses):
            def go(i=i, t=t):
                spread(0, t, i).start()
                spread(1, t, i).start()
            guarded(needed(me, u_peer(i), t), go)
        asked(t).start()

    for t in range(steps):
        tab_k[page_rows(me), t * kw:(t + 1) * kw] = krot[:, columns(me, t, kw)]
        qbuf[own_rows, t * qw:(t + 1) * qw] = qrot[:, columns(me, t, qw)]

    def onward(which, t, low):
        tab = (tab_k, tab_v)[which]
        count = (halo - low) * PAGE
        return pltpu.make_async_remote_copy(
            src_ref=tab.at[home + rows - count:home + rows, t * kw:(t + 1) * kw],
            dst_ref=tab.at[low * PAGE:halo * PAGE, t * kw:(t + 1) * kw],
            send_sem=x_send.at[which, t], recv_sem=x_recv.at[which, t],
            device_id={"blk": lax.rem(blk + 1, blks)}, device_id_type=MESH,
        )

    def each_halo(condition, action):
        for d in range(ulysses // 2):
            if 2 * d < halo:
                pl.when(condition & (duo == d))(functools.partial(action, 2 * d))

    def page_for(owner):
        def step(j, found):
            page = table_ref[pack, blk * ulysses + j]
            return found + jnp.where(lax.div(page, jnp.int32(ulysses)) == owner, j, 0)
        return lax.fori_loop(0, ulysses, step, jnp.int32(0))

    def handed(which, i):
        src, dst = ((out_k, got_k), (out_v, got_v))[which]
        return pltpu.make_async_remote_copy(
            src_ref=src.at[i], dst_ref=dst.at[mine],
            send_sem=c_send.at[which, i - 1], recv_sem=c_recv.at[which, i - 1],
            device_id=s_peer(i)[1], device_id_type=MESH,
        )

    def own_page(which):
        src, dst = ((out_k, got_k), (out_v, got_v))[which]
        return pltpu.make_async_copy(src.at[0], dst.at[mine], c_local.at[which])

    def hand_over():
        for i in range(sources):
            chosen = page_for(s_peer(i)[0])
            for tab, out in ((tab_k, out_k), (tab_v, out_v)):
                for h in range(kvl):
                    out[i, h] = pick(chosen, [
                        tab[home + j * PAGE:home + (j + 1) * PAGE, h * HD:(h + 1) * HD] for j in range(ulysses)
                    ])
        for i in range(1, sources):
            handed(0, i).start()
            handed(1, i).start()
        own_page(0).start()
        own_page(1).start()

    block = 2 * PAGE
    span = home + block
    factor = QUERY_SCALE / SOFT_CAP
    begin = pl.multiple_of(duo * block, block)
    seen = pl.ds(begin, span)
    q_pos = blk * rows + duo * block + lax.broadcasted_iota(jnp.int32, (block, 1), 0)
    q_low = jnp.maximum(first_token(q_pos), q_pos - (WINDOW - 1))
    key_pos = blk * rows - home + begin + lax.broadcasted_iota(jnp.int32, (1, span), 1)
    allowed = (key_pos <= q_pos) & (key_pos >= q_low)
    allowed = jnp.concatenate([allowed] * group, axis=0)

    def attend(h):
        query = jnp.concatenate(
            [qbuf[:, (h * group + g) * HD:(h * group + g + 1) * HD] for g in range(group)], axis=0
        )
        scores = lax.dot_general(
            query, tab_k[seen, h * HD:(h + 1) * HD], (((1,), (1,)), ((), ())), preferred_element_type=jnp.float32
        )
        weights = jnp.exp(SOFT_CAP * jnp.tanh(scores * factor))
        weights = jnp.where(allowed, weights, 0.0)
        total = jnp.sum(weights, axis=1, keepdims=True)
        mixed = jnp.dot(
            weights.astype(jnp.bfloat16), tab_v[seen, h * HD:(h + 1) * HD], preferred_element_type=jnp.float32
        )
        result = (mixed / total).astype(jnp.bfloat16)
        for g in range(group):
            obuf[:, (h * group + g) * HD:(h * group + g + 1) * HD] = result[g * block:(g + 1) * block]

    def outgoing(t):
        return pltpu.make_async_remote_copy(
            src_ref=obuf.at[mate_rows, t * qw:(t + 1) * qw],
            dst_ref=out_ref.at[:, columns(me, t, qw)],
            send_sem=o_send.at[t], recv_sem=o_recv.at[t],
            device_id={"ulysses": mate}, device_id_type=MESH,
        )

    for t in range(steps):
        own_values(t).wait()
        for i in range(1, ulysses):
            def landed(i=i, t=t):
                spread(0, t, i).wait_recv()
                spread(1, t, i).wait_recv()
            guarded(needed(u_source(i), me, t), landed)

        def send_on(low, t=t):
            onward(0, t, low).start()
            onward(1, t, low).start()

        def receive(low, t=t):
            onward(0, t, low).wait_recv()
            onward(1, t, low).wait_recv()

        each_halo(blk + 1 < blks, send_on)
        if t == inner - 1:
            hand_over()
        each_halo(blk > 0, receive)
        asked(t).wait_recv()
        for h in range(t * per, (t + 1) * per):
            attend(h)
        outgoing(t).start()
        out_ref[:, columns(me, t, qw)] = obuf[own_rows, t * qw:(t + 1) * qw]

    own_page(0).wait()
    own_page(1).wait()
    for i in range(1, sources):
        handed(0, i).wait_recv()
        handed(1, i).wait_recv()
    for j in range(ulysses):
        def step(n, found, j=j):
            s = n // ulysses
            page = table_ref[lax.rem(s, cores), (s // cores) * ulysses + lax.rem(n, ulysses)]
            return found + jnp.where(page == mine * ulysses + j, s, 0)
        source = lax.fori_loop(0, sources * ulysses, step, jnp.int32(0))
        ck_ref[j] = pick(source, [got_k[s] for s in range(sources)])
        cv_ref[j] = pick(source, [got_v[s] for s in range(sources)])

    for i in range(1, sources):
        handed(0, i).wait_send()
        handed(1, i).wait_send()
    for t in range(steps):
        for i in range(1, ulysses):
            def sent(i=i, t=t):
                spread(0, t, i).wait_send()
                spread(1, t, i).wait_send()
            guarded(needed(me, u_peer(i), t), sent)
        asked(t).wait_send()

        def passed(low, t=t):
            onward(0, t, low).wait_send()
            onward(1, t, low).wait_send()

        each_halo(blk + 1 < blks, passed)
        outgoing(t).wait()


def place(*refs):
    count = (len(refs) - 1) // 2
    sem = refs[-1]
    copies = [pltpu.make_async_copy(refs[i], refs[count + i], sem.at[i]) for i in range(count)]
    for copy in copies:
        copy.start()
    for copy in copies:
        copy.wait()


def body(queries, keys, values, request_pages, page_table):
    local = queries.shape[1]
    ulysses = lax.axis_size("ulysses")
    blks = lax.axis_size("blk")
    cores = lax.axis_size("handoff")
    kvl = KVH // ulysses
    group = QH // KVH
    rows = local * ulysses
    slots = rows // PAGE
    sources = blks * cores
    assert slots == sources
    reach = min(WINDOW, page_table.shape[1] // 2 * PAGE)
    back = min(-(-reach // rows), blks - 1)
    reqs = request_pages.shape[1]
    half = np.arange(HD // 2, dtype=np.float64)
    freq = (ROPE_BASE ** (-2.0 * half / HD)).astype(np.float32)
    freq = jnp.asarray(np.concatenate([freq, freq])[None, :])
    sizes = (ulysses, blks, cores, local, kvl, group, reach, reqs)
    qw = group * HD
    halo = reach // PAGE - 1
    per = min(1, kvl)
    bf = jnp.bfloat16
    dma = pltpu.SemaphoreType.DMA
    hops = max(back, 1)
    anywhere = pl.BlockSpec(memory_space=pl.ANY)
    vmem = pl.BlockSpec(memory_space=pltpu.VMEM)
    smem = pl.BlockSpec(memory_space=pltpu.SMEM)
    narrow = local == PAGE and ulysses % 2 == 0 and 0 < halo <= ulysses and kvl % per == 0 and blks > 1
    if narrow:
        held = ulysses // 2 * kvl
        steps = held // per
        run = functools.partial(paired, (ulysses, blks, cores, kvl, group, halo, reqs, per))
        table = pltpu.VMEM((halo * PAGE + rows, held * HD), bf)
        handing = pltpu.VMEM((sources, kvl, PAGE, HD), bf)
        scratch = [
            pltpu.VMEM((PAGE, QH * HD), bf),
            pltpu.VMEM((PAGE, KVH * HD), bf),
            pltpu.VMEM((PAGE, QH * HD), bf),
            pltpu.VMEM((PAGE, KVH * HD), bf),
            table, table,
            pltpu.VMEM((2 * PAGE, held * qw), bf),
            pltpu.VMEM((2 * PAGE, held * qw), bf),
            handing, handing, handing, handing,
            dma((2,)),
            dma((2, steps, ulysses - 1)),
            dma((2, steps, ulysses - 1)),
            dma((steps,)),
            dma((steps,)),
            dma((steps,)),
            dma((2, steps)),
            dma((2, steps)),
            dma((2, sources - 1)),
            dma((2, sources - 1)),
            dma((2,)),
            dma((steps,)),
            dma((steps,)),
        ]
    else:
        run = functools.partial(kernel, sizes)
        scratch = [
            pltpu.VMEM((kvl, rows, HD), bf),
            pltpu.VMEM((kvl, (back + 1) * rows, HD), bf),
            pltpu.VMEM((kvl, (back + 1) * rows, HD), bf),
            pltpu.VMEM((kvl, rows, qw), bf),
            pltpu.VMEM((kvl, rows, qw), bf),
            pltpu.VMEM((rows, HD), jnp.float32),
            pltpu.VMEM((rows, HD), jnp.float32),
            pltpu.VMEM((sources, kvl, PAGE, HD), bf),
            pltpu.VMEM((sources, kvl, PAGE, HD), bf),
            pltpu.VMEM((sources, kvl, PAGE, HD), bf),
            pltpu.VMEM((sources, kvl, PAGE, HD), bf),
            dma((3, kvl, ulysses - 1)),
            dma((3, kvl, ulysses - 1)),
            dma((3, kvl)),
            dma((2, kvl, hops)),
            dma((2, kvl, hops)),
            dma((2, sources - 1)),
            dma((2, sources - 1)),
            dma((2,)),
            dma((kvl, ulysses - 1)),
            dma((kvl, ulysses - 1)),
            dma((kvl,)),
        ]
    results = pl.pallas_call(
        run,
        out_shape=(
            pltpu.VMEM((local, QH * HD), bf),
            pltpu.VMEM((slots, kvl, PAGE, HD), bf),
            pltpu.VMEM((slots, kvl, PAGE, HD), bf),
        ),
        in_specs=[anywhere, anywhere, anywhere, vmem, smem, smem],
        out_specs=(vmem, vmem, vmem),
        scratch_shapes=scratch,
        compiler_params=pltpu.CompilerParams(collective_id=0, has_side_effects=True),
    )(queries[0], keys[0], values[0], freq, request_pages, page_table)
    results = [pltpu.with_memory_space_constraint(x, pltpu.VMEM) for x in results]
    attended, cache_keys, cache_values = pl.pallas_call(
        place,
        out_shape=tuple(jax.ShapeDtypeStruct(x.shape, x.dtype) for x in results),
        in_specs=[anywhere] * len(results),
        out_specs=(anywhere,) * len(results),
        scratch_shapes=[dma((len(results),))],
        compiler_params=pltpu.CompilerParams(vmem_limit_bytes=1 << 20),
    )(*results)
    return (attended[None], cache_keys, cache_values)


def solution(mesh):
    in_specs = (
        P(("groups", "handoff"), ("blk", "ulysses"), None),
        P(("groups", "handoff"), ("blk", "ulysses"), None),
        P(("groups", "handoff"), ("blk", "ulysses"), None),
        P("groups", None),
        P("groups", None),
    )
    out_specs = (
        P(("groups", "handoff"), ("blk", "ulysses"), None),
        P(("groups", "blk", "handoff"), "ulysses", None, None),
        P(("groups", "blk", "handoff"), "ulysses", None, None),
    )
    return jax.shard_map(body, mesh=mesh, in_specs=in_specs, out_specs=out_specs, check_vma=False)
```

```python
import functools

import jax
import jax.numpy as jnp
import numpy as np
from jax import lax
from jax.experimental import pallas as pl
from jax.experimental.pallas import tpu as pltpu
from jax.sharding import PartitionSpec as P

QH = 32
KVH = 16
HD = 128
WINDOW = 4096
PAGE = 64

QUERY_SCALE = 144.0 ** (-0.5)
SOFT_CAP = 50.0
ROPE_BASE = 10000.0
MESH = pl.DeviceIdType.MESH
LAG = 1


def turn(x, cosine, sine):
    wide = x.astype(jnp.float32)
    return (wide * cosine + pltpu.roll(wide, HD // 2, 1) * sine).astype(jnp.bfloat16)


def pick(index, choices):
    chosen = choices[0]
    for j in range(1, len(choices)):
        chosen = jnp.where(index == j, choices[j], chosen)
    return chosen


def kernel(
    sizes, q_ref, k_ref, v_ref, freq_ref, pages_ref, table_ref,
    out_ref, ck_ref, cv_ref,
    kraw, tab_k, tab_v, qbuf, obuf, cos_t, sin_t, out_k, out_v, got_k, got_v,
    in_send, in_recv, in_local, x_send, x_recv, c_send, c_recv, c_local, o_send, o_recv, o_local,
):
    ulysses, blks, cores, local, kvl, group, reach, reqs = sizes
    rows = ulysses * local
    slots = rows // PAGE
    sources = blks * cores
    back = min(-(-reach // rows), blks - 1)
    home = back * rows
    qw = group * HD
    me = lax.axis_index("ulysses")
    blk = lax.axis_index("blk")
    pack = lax.axis_index("handoff")
    mine = blk * cores + pack

    barrier = pltpu.get_barrier_semaphore()

    def u_peer(i):
        return lax.rem(me + i, ulysses)

    def s_peer(i):
        p = lax.rem(mine + i, sources)
        return p, {"blk": p // cores, "handoff": lax.rem(p, cores)}

    for i in range(1, ulysses):
        pl.semaphore_signal(barrier, inc=1, device_id={"ulysses": u_peer(i)}, device_id_type=MESH)
    for i in range(1, sources):
        pl.semaphore_signal(barrier, inc=1, device_id=s_peer(i)[1], device_id_type=MESH)

    for hop in range(1, back + 1):
        @pl.when(blk < hop)
        def _():
            part = pl.ds((back - hop) * rows, rows)
            tab_k[:, part, :] = jnp.zeros((kvl, rows, HD), jnp.bfloat16)
            tab_v[:, part, :] = jnp.zeros((kvl, rows, HD), jnp.bfloat16)

    pl.semaphore_wait(barrier, ulysses - 1 + sources - 1)

    def landing(what, h, whose):
        if what == 0:
            return kraw.at[h, pl.ds(whose * local, local), :]
        if what == 1:
            return tab_v.at[h, pl.ds(home + whose * local, local), :]
        return qbuf.at[h, pl.ds(whose * local, local), :]

    def leaving(what, h, whose):
        width = qw if what == 2 else HD
        ref = (k_ref, v_ref, q_ref)[what]
        return ref.at[:, pl.ds(pl.multiple_of((whose * kvl + h) * width, width), width)]

    def incoming(what, h, i):
        return pltpu.make_async_remote_copy(
            src_ref=leaving(what, h, u_peer(i)), dst_ref=landing(what, h, me),
            send_sem=in_send.at[what, h, i - 1], recv_sem=in_recv.at[what, h, i - 1],
            device_id={"ulysses": u_peer(i)}, device_id_type=MESH,
        )

    def own_in(what, h):
        return pltpu.make_async_copy(leaving(what, h, me), landing(what, h, me), in_local.at[what, h])

    order = [(w, h) for h in range(kvl) for w in (0, 1)] + [(2, h) for h in range(kvl)]
    for what, h in order:
        for i in range(1, ulysses):
            incoming(what, h, i).start()
        own_in(what, h).start()

    def arrive(what, h):
        own_in(what, h).wait()
        for i in range(1, ulysses):
            incoming(what, h, i).wait_recv()

    ends = []
    starts = []
    total = jnp.int32(0)
    for r in range(reqs):
        starts.append(total)
        total = total + pages_ref[pack, r] * PAGE
        ends.append(total)

    def first_token(pos):
        first = jnp.zeros_like(pos)
        for r in range(reqs):
            first = jnp.maximum(first, jnp.where(pos >= starts[r], starts[r], 0))
        return first

    pos_rows = blk * rows + lax.broadcasted_iota(jnp.int32, (rows, HD), 0)
    rel = (pos_rows - first_token(pos_rows)).astype(jnp.float32)
    angles = rel * freq_ref[...]
    lanes = lax.broadcasted_iota(jnp.int32, (rows, HD), 1)
    cos_t[...] = jnp.cos(angles)
    sine = jnp.sin(angles)
    sin_t[...] = jnp.where(lanes < HD // 2, -sine, sine)

    def onward(which, h, hop):
        tab = (tab_k, tab_v)[which]
        return pltpu.make_async_remote_copy(
            src_ref=tab.at[h, pl.ds(home, rows), :],
            dst_ref=tab.at[h, pl.ds((back - hop) * rows, rows), :],
            send_sem=x_send.at[which, h, hop - 1], recv_sem=x_recv.at[which, h, hop - 1],
            device_id={"blk": lax.rem(blk + hop, blks)}, device_id_type=MESH,
        )

    for h in range(kvl):
        arrive(0, h)
        tab_k[h, pl.ds(home, rows), :] = turn(kraw[h], cos_t[...], sin_t[...])
        arrive(1, h)
        for hop in range(1, back + 1):
            @pl.when(blk + hop < blks)
            def _():
                onward(0, h, hop).start()
                onward(1, h, hop).start()

    def page_for(owner):
        def step(j, found):
            page = table_ref[pack, blk * slots + j]
            return found + jnp.where(lax.div(page, jnp.int32(slots)) == owner, j, 0)
        return lax.fori_loop(0, slots, step, jnp.int32(0))

    def handed(which, i):
        src, dst = ((out_k, got_k), (out_v, got_v))[which]
        return pltpu.make_async_remote_copy(
            src_ref=src.at[i], dst_ref=dst.at[mine],
            send_sem=c_send.at[which, i - 1], recv_sem=c_recv.at[which, i - 1],
            device_id=s_peer(i)[1], device_id_type=MESH,
        )

    def own_page(which):
        src, dst = ((out_k, got_k), (out_v, got_v))[which]
        return pltpu.make_async_copy(src.at[0], dst.at[mine], c_local.at[which])

    for i in range(sources):
        chosen = page_for(s_peer(i)[0])
        for tab, out in ((tab_k, out_k), (tab_v, out_v)):
            out[i] = pick(chosen, [tab[:, home + j * PAGE:home + (j + 1) * PAGE, :] for j in range(slots)])
    for i in range(1, sources):
        handed(0, i).start()
        handed(1, i).start()
    own_page(0).start()
    own_page(1).start()

    block = min(rows, 128)
    lead = min(-(-reach // block) * block, home)
    span = lead + block
    chunk = span if span <= 512 else block
    factor = QUERY_SCALE / SOFT_CAP

    def attend(h, i):
        at = i * block
        if not isinstance(i, int):
            at = pl.multiple_of(at, block)
        here = pl.ds(at, block)
        cosine, sine_here = cos_t[here, :], sin_t[here, :]
        query = jnp.concatenate(
            [turn(qbuf[h, here, g * HD:(g + 1) * HD], cosine, sine_here) for g in range(group)], axis=0
        )
        pos = blk * rows + at + lax.broadcasted_iota(jnp.int32, (block, 1), 0)
        low = jnp.maximum(first_token(pos), pos - (WINDOW - 1))
        pos = jnp.concatenate([pos] * group, axis=0)
        low = jnp.concatenate([low] * group, axis=0)
        begin = home + at - lead

        def part(c):
            start = begin + c * chunk
            if not isinstance(start, int):
                start = pl.multiple_of(start, block)
            seen = pl.ds(start, chunk)
            scores = lax.dot_general(
                query, tab_k[h, seen, :], (((1,), (1,)), ((), ())), preferred_element_type=jnp.float32
            )
            weights = jnp.exp(SOFT_CAP * jnp.tanh(scores * factor))
            key_pos = (blk - back) * rows + start + lax.broadcasted_iota(jnp.int32, (1, chunk), 1)
            weights = jnp.where((key_pos <= pos) & (key_pos >= low), weights, 0.0)
            total = jnp.sum(weights, axis=1, keepdims=True)
            mixed = jnp.dot(
                weights.astype(jnp.bfloat16), tab_v[h, seen, :], preferred_element_type=jnp.float32
            )
            return mixed, total

        if span == chunk:
            mixed, total = part(0)
        else:
            def step(c, carry):
                mixed, total = part(c)
                return carry[0] + mixed, carry[1] + total
            mixed, total = lax.fori_loop(
                0, span // chunk, step,
                (jnp.zeros((group * block, HD), jnp.float32), jnp.zeros((group * block, 1), jnp.float32)),
            )
        result = (mixed / total).astype(jnp.bfloat16)
        for g in range(group):
            obuf[h, here, g * HD:(g + 1) * HD] = result[g * block:(g + 1) * block]

    def outgoing(h, i):
        return pltpu.make_async_remote_copy(
            src_ref=obuf.at[h, pl.ds(pl.multiple_of(u_peer(i) * local, local), local), :],
            dst_ref=out_ref.at[:, pl.ds(pl.multiple_of((me * kvl + h) * qw, qw), qw)],
            send_sem=o_send.at[h, i - 1], recv_sem=o_recv.at[h, i - 1],
            device_id={"ulysses": u_peer(i)}, device_id_type=MESH,
        )

    def own_out(h):
        return pltpu.make_async_copy(
            obuf.at[h, pl.ds(pl.multiple_of(me * local, local), local), :],
            out_ref.at[:, pl.ds(pl.multiple_of((me * kvl + h) * qw, qw), qw)],
            o_local.at[h],
        )

    for h in range(kvl):
        for hop in range(1, back + 1):
            @pl.when(blk >= hop)
            def _():
                onward(0, h, hop).wait_recv()
                onward(1, h, hop).wait_recv()
        arrive(2, h)
        if rows // block <= 4:
            for i in range(rows // block):
                attend(h, i)
        else:
            def each(i, carry):
                attend(h, i)
                return carry
            lax.fori_loop(0, rows // block, each, 0)
        for i in range(1, ulysses):
            outgoing(h, i).start()
        own_out(h).start()

    own_page(0).wait()
    own_page(1).wait()
    for i in range(1, sources):
        handed(0, i).wait_recv()
        handed(1, i).wait_recv()
    for j in range(slots):
        def step(n, found, j=j):
            s = n // slots
            page = table_ref[lax.rem(s, cores), (s // cores) * slots + lax.rem(n, slots)]
            return found + jnp.where(page == mine * slots + j, s, 0)
        source = lax.fori_loop(0, sources * slots, step, jnp.int32(0))
        ck_ref[j] = pick(source, [got_k[s] for s in range(sources)])
        cv_ref[j] = pick(source, [got_v[s] for s in range(sources)])

    for i in range(1, sources):
        handed(0, i).wait_send()
        handed(1, i).wait_send()
    for what, h in order:
        for i in range(1, ulysses):
            incoming(what, h, i).wait_send()
    for h in range(kvl):
        for hop in range(1, back + 1):
            @pl.when(blk + hop < blks)
            def _():
                onward(0, h, hop).wait_send()
                onward(1, h, hop).wait_send()
    for h in range(kvl):
        own_out(h).wait()
        for i in range(1, ulysses):
            outgoing(h, i).wait()


def paired(
    sizes, q_ref, k_ref, v_ref, freq_ref, pages_ref, table_ref,
    out_ref, ck_ref, cv_ref,
    qraw, kraw, qrot, krot, tab_k, tab_v, qbuf, obuf, out_k, out_v, got_k, got_v,
    load_sem, kv_send, kv_recv, v_local, q_send, q_recv, x_send, x_recv, c_send, c_recv, c_local, o_send, o_recv,
):
    ulysses, blks, cores, kvl, group, halo, reqs, per = sizes
    rows = ulysses * PAGE
    sources = blks * cores
    home = halo * PAGE
    picks = ulysses // 2
    steps = picks * kvl // per
    inner = kvl // per
    kw = per * HD
    qw = per * group * HD
    me = lax.axis_index("ulysses")
    blk = lax.axis_index("blk")
    pack = lax.axis_index("handoff")
    mine = blk * cores + pack
    side = lax.rem(me, 2)
    duo = lax.div(me, 2)
    mate = me + 1 - 2 * side

    loads = [
        pltpu.make_async_copy(k_ref, kraw, load_sem.at[0]),
        pltpu.make_async_copy(q_ref, qraw, load_sem.at[1]),
    ]
    for load in loads:
        load.start()

    barrier = pltpu.get_barrier_semaphore()

    def u_peer(i):
        return lax.rem(me + i, ulysses)

    def u_source(i):
        return lax.rem(me + ulysses - i, ulysses)

    def s_peer(i):
        p = lax.rem(mine + i, sources)
        return p, {"blk": p // cores, "handoff": lax.rem(p, cores)}

    for i in range(1, ulysses):
        pl.semaphore_signal(barrier, inc=1, device_id={"ulysses": u_peer(i)}, device_id_type=MESH)
    for i in range(1, sources):
        pl.semaphore_signal(barrier, inc=1, device_id=s_peer(i)[1], device_id_type=MESH)

    def columns(whose, t, width):
        chosen = lax.rem(whose + 2 * (t // inner), ulysses)
        return pl.ds(pl.multiple_of((chosen * inner + t % inner) * width, width), width)

    def page_rows(page):
        return pl.ds(pl.multiple_of(home + page * PAGE, PAGE), PAGE)

    own_rows = pl.ds(pl.multiple_of(side * PAGE, PAGE), PAGE)
    mate_rows = pl.ds(pl.multiple_of((1 - side) * PAGE, PAGE), PAGE)

    def own_values(t):
        return pltpu.make_async_copy(
            v_ref.at[:, columns(me, t, kw)], tab_v.at[page_rows(me), t * kw:(t + 1) * kw], v_local.at[t]
        )

    for t in range(steps):
        own_values(t).start()

    @pl.when(blk == 0)
    def _():
        tab_k[0:home, :] = jnp.zeros((home, steps * kw), jnp.bfloat16)
        tab_v[0:home, :] = jnp.zeros((home, steps * kw), jnp.bfloat16)

    starts = []
    total = jnp.int32(0)
    for r in range(reqs):
        starts.append(total)
        total = total + pages_ref[pack, r] * PAGE

    def first_token(pos):
        first = jnp.zeros_like(pos)
        for r in range(reqs):
            first = jnp.maximum(first, jnp.where(pos >= starts[r], starts[r], 0))
        return first

    pos = blk * rows + me * PAGE + lax.broadcasted_iota(jnp.int32, (PAGE, HD), 0)
    angles = (pos - first_token(pos)).astype(jnp.float32) * freq_ref[...]
    lanes = lax.broadcasted_iota(jnp.int32, (PAGE, HD), 1)
    cosine = jnp.cos(angles)
    sine = jnp.sin(angles)
    sine = jnp.where(lanes < HD // 2, -sine, sine)

    loads[0].wait()
    for h in range(KVH):
        at = slice(h * HD, (h + 1) * HD)
        krot[:, at] = turn(kraw[:, at], cosine, sine)
    loads[1].wait()
    for h in range(KVH * group):
        at = slice(h * HD, (h + 1) * HD)
        qrot[:, at] = turn(qraw[:, at], cosine, sine)

    pl.semaphore_wait(barrier, ulysses - 1 + sources - 1)

    def needed(page, reader, t):
        if t < inner:
            return None
        lower = page <= 2 * lax.div(reader, 2) + 1
        return lower | (blk + 1 < blks)

    def guarded(condition, action):
        if condition is None:
            action()
        else:
            pl.when(condition)(action)

    def spread(which, t, i):
        src = (krot, v_ref)[which]
        tab = (tab_k, tab_v)[which]
        return pltpu.make_async_remote_copy(
            src_ref=src.at[:, columns(u_peer(i), t, kw)],
            dst_ref=tab.at[page_rows(me), t * kw:(t + 1) * kw],
            send_sem=kv_send.at[which, t, i - 1], recv_sem=kv_recv.at[which, t, i - 1],
            device_id={"ulysses": u_peer(i)}, device_id_type=MESH,
        )

    def asked(t):
        return pltpu.make_async_remote_copy(
            src_ref=qrot.at[:, columns(mate, t, qw)],
            dst_ref=qbuf.at[own_rows, t * qw:(t + 1) * qw],
            send_sem=q_send.at[t], recv_sem=q_recv.at[t],
            device_id={"ulysses": mate}, device_id_type=MESH,
        )

    for t in range(steps):
        asked(t).start()
        for i in range(1, ulysses):
            def go(i=i, t=t):
                spread(0, t, i).start()
                spread(1, t, i).start()
            guarded(needed(me, u_peer(i), t), go)

    for t in range(steps):
        tab_k[page_rows(me), t * kw:(t + 1) * kw] = krot[:, columns(me, t, kw)]
        qbuf[own_rows, t * qw:(t + 1) * qw] = qrot[:, columns(me, t, qw)]

    def onward(which, t, low):
        tab = (tab_k, tab_v)[which]
        count = (halo - low) * PAGE
        return pltpu.make_async_remote_copy(
            src_ref=tab.at[home + rows - count:home + rows, t * kw:(t + 1) * kw],
            dst_ref=tab.at[low * PAGE:halo * PAGE, t * kw:(t + 1) * kw],
            send_sem=x_send.at[which, t], recv_sem=x_recv.at[which, t],
            device_id={"blk": lax.rem(blk + 1, blks)}, device_id_type=MESH,
        )

    def each_halo(condition, action):
        for d in range(ulysses // 2):
            if 2 * d < halo:
                pl.when(condition & (duo == d))(functools.partial(action, 2 * d))

    def page_for(owner):
        def step(j, found):
            page = table_ref[pack, blk * ulysses + j]
            return found + jnp.where(lax.div(page, jnp.int32(ulysses)) == owner, j, 0)
        return lax.fori_loop(0, ulysses, step, jnp.int32(0))

    def handed(which, i):
        src, dst = ((out_k, got_k), (out_v, got_v))[which]
        return pltpu.make_async_remote_copy(
            src_ref=src.at[i], dst_ref=dst.at[mine],
            send_sem=c_send.at[which, i - 1], recv_sem=c_recv.at[which, i - 1],
            device_id=s_peer(i)[1], device_id_type=MESH,
        )

    def own_page(which):
        src, dst = ((out_k, got_k), (out_v, got_v))[which]
        return pltpu.make_async_copy(src.at[0], dst.at[mine], c_local.at[which])

    def hand_over():
        for i in range(sources):
            chosen = page_for(s_peer(i)[0])
            for tab, out in ((tab_k, out_k), (tab_v, out_v)):
                for h in range(kvl):
                    out[i, h] = pick(chosen, [
                        tab[home + j * PAGE:home + (j + 1) * PAGE, h * HD:(h + 1) * HD] for j in range(ulysses)
                    ])
        for i in range(1, sources):
            handed(0, i).start()
            handed(1, i).start()
        own_page(0).start()
        own_page(1).start()

    block = 2 * PAGE
    span = home + block
    factor = QUERY_SCALE / SOFT_CAP
    begin = pl.multiple_of(duo * block, block)
    seen = pl.ds(begin, span)
    q_pos = blk * rows + duo * block + lax.broadcasted_iota(jnp.int32, (block, 1), 0)
    q_low = jnp.maximum(first_token(q_pos), q_pos - (WINDOW - 1))
    key_pos = blk * rows - home + begin + lax.broadcasted_iota(jnp.int32, (1, span), 1)
    allowed = (key_pos <= q_pos) & (key_pos >= q_low)
    allowed = jnp.concatenate([allowed] * group, axis=0)

    def attend(h):
        query = jnp.concatenate(
            [qbuf[:, (h * group + g) * HD:(h * group + g + 1) * HD] for g in range(group)], axis=0
        )
        scores = lax.dot_general(
            query, tab_k[seen, h * HD:(h + 1) * HD], (((1,), (1,)), ((), ())), preferred_element_type=jnp.float32
        )
        weights = jnp.exp(SOFT_CAP * jnp.tanh(scores * factor))
        weights = jnp.where(allowed, weights, 0.0)
        total = jnp.sum(weights, axis=1, keepdims=True)
        mixed = jnp.dot(
            weights.astype(jnp.bfloat16), tab_v[seen, h * HD:(h + 1) * HD], preferred_element_type=jnp.float32
        )
        result = (mixed / total).astype(jnp.bfloat16)
        for g in range(group):
            obuf[:, (h * group + g) * HD:(h * group + g + 1) * HD] = result[g * block:(g + 1) * block]

    def outgoing(t):
        return pltpu.make_async_remote_copy(
            src_ref=obuf.at[mate_rows, t * qw:(t + 1) * qw],
            dst_ref=out_ref.at[:, columns(me, t, qw)],
            send_sem=o_send.at[t], recv_sem=o_recv.at[t],
            device_id={"ulysses": mate}, device_id_type=MESH,
        )

    def relay(t):
        own_values(t).wait()
        for i in range(1, ulysses):
            def landed(i=i):
                spread(0, t, i).wait_recv()
                spread(1, t, i).wait_recv()
            guarded(needed(u_source(i), me, t), landed)

        def send_on(low):
            onward(0, t, low).start()
            onward(1, t, low).start()

        each_halo(blk + 1 < blks, send_on)
        if t == inner - 1:
            hand_over()

    def work(t):
        def receive(low):
            onward(0, t, low).wait_recv()
            onward(1, t, low).wait_recv()

        each_halo(blk > 0, receive)
        asked(t).wait_recv()
        for h in range(t * per, (t + 1) * per):
            attend(h)
        outgoing(t).start()
        out_ref[:, columns(me, t, qw)] = obuf[own_rows, t * qw:(t + 1) * qw]

    for t in range(steps + LAG):
        if t < steps:
            relay(t)
        if t >= LAG:
            work(t - LAG)

    own_page(0).wait()
    own_page(1).wait()
    for i in range(1, sources):
        handed(0, i).wait_recv()
        handed(1, i).wait_recv()
    for j in range(ulysses):
        def step(n, found, j=j):
            s = n // ulysses
            page = table_ref[lax.rem(s, cores), (s // cores) * ulysses + lax.rem(n, ulysses)]
            return found + jnp.where(page == mine * ulysses + j, s, 0)
        source = lax.fori_loop(0, sources * ulysses, step, jnp.int32(0))
        ck_ref[j] = pick(source, [got_k[s] for s in range(sources)])
        cv_ref[j] = pick(source, [got_v[s] for s in range(sources)])

    for i in range(1, sources):
        handed(0, i).wait_send()
        handed(1, i).wait_send()
    for t in range(steps):
        for i in range(1, ulysses):
            def sent(i=i, t=t):
                spread(0, t, i).wait_send()
                spread(1, t, i).wait_send()
            guarded(needed(me, u_peer(i), t), sent)
        asked(t).wait_send()

        def passed(low, t=t):
            onward(0, t, low).wait_send()
            onward(1, t, low).wait_send()

        each_halo(blk + 1 < blks, passed)
        outgoing(t).wait()


def place(*refs):
    count = (len(refs) - 1) // 2
    sem = refs[-1]
    copies = [pltpu.make_async_copy(refs[i], refs[count + i], sem.at[i]) for i in range(count)]
    for copy in copies:
        copy.start()
    for copy in copies:
        copy.wait()


def body(queries, keys, values, request_pages, page_table):
    local = queries.shape[1]
    ulysses = lax.axis_size("ulysses")
    blks = lax.axis_size("blk")
    cores = lax.axis_size("handoff")
    kvl = KVH // ulysses
    group = QH // KVH
    rows = local * ulysses
    slots = rows // PAGE
    sources = blks * cores
    assert slots == sources
    reach = min(WINDOW, page_table.shape[1] // 2 * PAGE)
    back = min(-(-reach // rows), blks - 1)
    reqs = request_pages.shape[1]
    half = np.arange(HD // 2, dtype=np.float64)
    freq = (ROPE_BASE ** (-2.0 * half / HD)).astype(np.float32)
    freq = jnp.asarray(np.concatenate([freq, freq])[None, :])
    sizes = (ulysses, blks, cores, local, kvl, group, reach, reqs)
    qw = group * HD
    halo = reach // PAGE - 1
    per = min(1, kvl)
    bf = jnp.bfloat16
    dma = pltpu.SemaphoreType.DMA
    hops = max(back, 1)
    anywhere = pl.BlockSpec(memory_space=pl.ANY)
    vmem = pl.BlockSpec(memory_space=pltpu.VMEM)
    smem = pl.BlockSpec(memory_space=pltpu.SMEM)
    narrow = local == PAGE and ulysses % 2 == 0 and 0 < halo <= ulysses and kvl % per == 0 and blks > 1
    if narrow:
        held = ulysses // 2 * kvl
        steps = held // per
        run = functools.partial(paired, (ulysses, blks, cores, kvl, group, halo, reqs, per))
        table = pltpu.VMEM((halo * PAGE + rows, held * HD), bf)
        handing = pltpu.VMEM((sources, kvl, PAGE, HD), bf)
        scratch = [
            pltpu.VMEM((PAGE, QH * HD), bf),
            pltpu.VMEM((PAGE, KVH * HD), bf),
            pltpu.VMEM((PAGE, QH * HD), bf),
            pltpu.VMEM((PAGE, KVH * HD), bf),
            table, table,
            pltpu.VMEM((2 * PAGE, held * qw), bf),
            pltpu.VMEM((2 * PAGE, held * qw), bf),
            handing, handing, handing, handing,
            dma((2,)),
            dma((2, steps, ulysses - 1)),
            dma((2, steps, ulysses - 1)),
            dma((steps,)),
            dma((steps,)),
            dma((steps,)),
            dma((2, steps)),
            dma((2, steps)),
            dma((2, sources - 1)),
            dma((2, sources - 1)),
            dma((2,)),
            dma((steps,)),
            dma((steps,)),
        ]
    else:
        run = functools.partial(kernel, sizes)
        scratch = [
            pltpu.VMEM((kvl, rows, HD), bf),
            pltpu.VMEM((kvl, (back + 1) * rows, HD), bf),
            pltpu.VMEM((kvl, (back + 1) * rows, HD), bf),
            pltpu.VMEM((kvl, rows, qw), bf),
            pltpu.VMEM((kvl, rows, qw), bf),
            pltpu.VMEM((rows, HD), jnp.float32),
            pltpu.VMEM((rows, HD), jnp.float32),
            pltpu.VMEM((sources, kvl, PAGE, HD), bf),
            pltpu.VMEM((sources, kvl, PAGE, HD), bf),
            pltpu.VMEM((sources, kvl, PAGE, HD), bf),
            pltpu.VMEM((sources, kvl, PAGE, HD), bf),
            dma((3, kvl, ulysses - 1)),
            dma((3, kvl, ulysses - 1)),
            dma((3, kvl)),
            dma((2, kvl, hops)),
            dma((2, kvl, hops)),
            dma((2, sources - 1)),
            dma((2, sources - 1)),
            dma((2,)),
            dma((kvl, ulysses - 1)),
            dma((kvl, ulysses - 1)),
            dma((kvl,)),
        ]
    results = pl.pallas_call(
        run,
        out_shape=(
            pltpu.VMEM((local, QH * HD), bf),
            pltpu.VMEM((slots, kvl, PAGE, HD), bf),
            pltpu.VMEM((slots, kvl, PAGE, HD), bf),
        ),
        in_specs=[anywhere, anywhere, anywhere, vmem, smem, smem],
        out_specs=(vmem, vmem, vmem),
        scratch_shapes=scratch,
        compiler_params=pltpu.CompilerParams(collective_id=0, has_side_effects=True),
    )(queries[0], keys[0], values[0], freq, request_pages, page_table)
    results = [pltpu.with_memory_space_constraint(x, pltpu.VMEM) for x in results]
    attended, cache_keys, cache_values = pl.pallas_call(
        place,
        out_shape=tuple(jax.ShapeDtypeStruct(x.shape, x.dtype) for x in results),
        in_specs=[anywhere] * len(results),
        out_specs=(anywhere,) * len(results),
        scratch_shapes=[dma((len(results),))],
        compiler_params=pltpu.CompilerParams(vmem_limit_bytes=1 << 20),
    )(*results)
    return (attended[None], cache_keys, cache_values)


def solution(mesh):
    in_specs = (
        P(("groups", "handoff"), ("blk", "ulysses"), None),
        P(("groups", "handoff"), ("blk", "ulysses"), None),
        P(("groups", "handoff"), ("blk", "ulysses"), None),
        P("groups", None),
        P("groups", None),
    )
    out_specs = (
        P(("groups", "handoff"), ("blk", "ulysses"), None),
        P(("groups", "blk", "handoff"), "ulysses", None, None),
        P(("groups", "blk", "handoff"), "ulysses", None, None),
    )
    return jax.shard_map(body, mesh=mesh, in_specs=in_specs, out_specs=out_specs, check_vma=False)
```

```python
import functools

import jax
import jax.numpy as jnp
import numpy as np
from jax import lax
from jax.experimental import pallas as pl
from jax.experimental.pallas import tpu as pltpu
from jax.sharding import PartitionSpec as P

QH = 32
KVH = 16
HD = 128
WINDOW = 4096
PAGE = 64

QUERY_SCALE = 144.0 ** (-0.5)
SOFT_CAP = 50.0
ROPE_BASE = 10000.0
MESH = pl.DeviceIdType.MESH
LAG = 1


def turn(x, cosine, sine):
    wide = x.astype(jnp.float32)
    return (wide * cosine + pltpu.roll(wide, HD // 2, 1) * sine).astype(jnp.bfloat16)


def pick(index, choices):
    chosen = choices[0]
    for j in range(1, len(choices)):
        chosen = jnp.where(index == j, choices[j], chosen)
    return chosen


def kernel(
    sizes, q_ref, k_ref, v_ref, freq_ref, pages_ref, table_ref,
    out_ref, ck_ref, cv_ref,
    kraw, tab_k, tab_v, qbuf, obuf, cos_t, sin_t, out_k, out_v, got_k, got_v,
    in_send, in_recv, in_local, x_send, x_recv, c_send, c_recv, c_local, o_send, o_recv, o_local,
):
    ulysses, blks, cores, local, kvl, group, reach, reqs = sizes
    rows = ulysses * local
    slots = rows // PAGE
    sources = blks * cores
    back = min(-(-reach // rows), blks - 1)
    home = back * rows
    qw = group * HD
    me = lax.axis_index("ulysses")
    blk = lax.axis_index("blk")
    pack = lax.axis_index("handoff")
    mine = blk * cores + pack

    barrier = pltpu.get_barrier_semaphore()

    def u_peer(i):
        return lax.rem(me + i, ulysses)

    def s_peer(i):
        p = lax.rem(mine + i, sources)
        return p, {"blk": p // cores, "handoff": lax.rem(p, cores)}

    for i in range(1, ulysses):
        pl.semaphore_signal(barrier, inc=1, device_id={"ulysses": u_peer(i)}, device_id_type=MESH)
    for i in range(1, sources):
        pl.semaphore_signal(barrier, inc=1, device_id=s_peer(i)[1], device_id_type=MESH)

    for hop in range(1, back + 1):
        @pl.when(blk < hop)
        def _():
            part = pl.ds((back - hop) * rows, rows)
            tab_k[:, part, :] = jnp.zeros((kvl, rows, HD), jnp.bfloat16)
            tab_v[:, part, :] = jnp.zeros((kvl, rows, HD), jnp.bfloat16)

    pl.semaphore_wait(barrier, ulysses - 1 + sources - 1)

    def landing(what, h, whose):
        if what == 0:
            return kraw.at[h, pl.ds(whose * local, local), :]
        if what == 1:
            return tab_v.at[h, pl.ds(home + whose * local, local), :]
        return qbuf.at[h, pl.ds(whose * local, local), :]

    def leaving(what, h, whose):
        width = qw if what == 2 else HD
        ref = (k_ref, v_ref, q_ref)[what]
        return ref.at[:, pl.ds(pl.multiple_of((whose * kvl + h) * width, width), width)]

    def incoming(what, h, i):
        return pltpu.make_async_remote_copy(
            src_ref=leaving(what, h, u_peer(i)), dst_ref=landing(what, h, me),
            send_sem=in_send.at[what, h, i - 1], recv_sem=in_recv.at[what, h, i - 1],
            device_id={"ulysses": u_peer(i)}, device_id_type=MESH,
        )

    def own_in(what, h):
        return pltpu.make_async_copy(leaving(what, h, me), landing(what, h, me), in_local.at[what, h])

    order = [(w, h) for h in range(kvl) for w in (0, 1)] + [(2, h) for h in range(kvl)]
    for what, h in order:
        for i in range(1, ulysses):
            incoming(what, h, i).start()
        own_in(what, h).start()

    def arrive(what, h):
        own_in(what, h).wait()
        for i in range(1, ulysses):
            incoming(what, h, i).wait_recv()

    ends = []
    starts = []
    total = jnp.int32(0)
    for r in range(reqs):
        starts.append(total)
        total = total + pages_ref[pack, r] * PAGE
        ends.append(total)

    def first_token(pos):
        first = jnp.zeros_like(pos)
        for r in range(reqs):
            first = jnp.maximum(first, jnp.where(pos >= starts[r], starts[r], 0))
        return first

    pos_rows = blk * rows + lax.broadcasted_iota(jnp.int32, (rows, HD), 0)
    rel = (pos_rows - first_token(pos_rows)).astype(jnp.float32)
    angles = rel * freq_ref[...]
    lanes = lax.broadcasted_iota(jnp.int32, (rows, HD), 1)
    cos_t[...] = jnp.cos(angles)
    sine = jnp.sin(angles)
    sin_t[...] = jnp.where(lanes < HD // 2, -sine, sine)

    def onward(which, h, hop):
        tab = (tab_k, tab_v)[which]
        return pltpu.make_async_remote_copy(
            src_ref=tab.at[h, pl.ds(home, rows), :],
            dst_ref=tab.at[h, pl.ds((back - hop) * rows, rows), :],
            send_sem=x_send.at[which, h, hop - 1], recv_sem=x_recv.at[which, h, hop - 1],
            device_id={"blk": lax.rem(blk + hop, blks)}, device_id_type=MESH,
        )

    for h in range(kvl):
        arrive(0, h)
        tab_k[h, pl.ds(home, rows), :] = turn(kraw[h], cos_t[...], sin_t[...])
        arrive(1, h)
        for hop in range(1, back + 1):
            @pl.when(blk + hop < blks)
            def _():
                onward(0, h, hop).start()
                onward(1, h, hop).start()

    def page_for(owner):
        def step(j, found):
            page = table_ref[pack, blk * slots + j]
            return found + jnp.where(lax.div(page, jnp.int32(slots)) == owner, j, 0)
        return lax.fori_loop(0, slots, step, jnp.int32(0))

    def handed(which, i):
        src, dst = ((out_k, got_k), (out_v, got_v))[which]
        return pltpu.make_async_remote_copy(
            src_ref=src.at[i], dst_ref=dst.at[mine],
            send_sem=c_send.at[which, i - 1], recv_sem=c_recv.at[which, i - 1],
            device_id=s_peer(i)[1], device_id_type=MESH,
        )

    def own_page(which):
        src, dst = ((out_k, got_k), (out_v, got_v))[which]
        return pltpu.make_async_copy(src.at[0], dst.at[mine], c_local.at[which])

    for i in range(sources):
        chosen = page_for(s_peer(i)[0])
        for tab, out in ((tab_k, out_k), (tab_v, out_v)):
            out[i] = pick(chosen, [tab[:, home + j * PAGE:home + (j + 1) * PAGE, :] for j in range(slots)])
    for i in range(1, sources):
        handed(0, i).start()
        handed(1, i).start()
    own_page(0).start()
    own_page(1).start()

    block = min(rows, 128)
    lead = min(-(-reach // block) * block, home)
    span = lead + block
    chunk = span if span <= 512 else block
    factor = QUERY_SCALE / SOFT_CAP

    def attend(h, i):
        at = i * block
        if not isinstance(i, int):
            at = pl.multiple_of(at, block)
        here = pl.ds(at, block)
        cosine, sine_here = cos_t[here, :], sin_t[here, :]
        query = jnp.concatenate(
            [turn(qbuf[h, here, g * HD:(g + 1) * HD], cosine, sine_here) for g in range(group)], axis=0
        )
        pos = blk * rows + at + lax.broadcasted_iota(jnp.int32, (block, 1), 0)
        low = jnp.maximum(first_token(pos), pos - (WINDOW - 1))
        pos = jnp.concatenate([pos] * group, axis=0)
        low = jnp.concatenate([low] * group, axis=0)
        begin = home + at - lead

        def part(c):
            start = begin + c * chunk
            if not isinstance(start, int):
                start = pl.multiple_of(start, block)
            seen = pl.ds(start, chunk)
            scores = lax.dot_general(
                query, tab_k[h, seen, :], (((1,), (1,)), ((), ())), preferred_element_type=jnp.float32
            )
            weights = jnp.exp(SOFT_CAP * jnp.tanh(scores * factor))
            key_pos = (blk - back) * rows + start + lax.broadcasted_iota(jnp.int32, (1, chunk), 1)
            weights = jnp.where((key_pos <= pos) & (key_pos >= low), weights, 0.0)
            total = jnp.sum(weights, axis=1, keepdims=True)
            mixed = jnp.dot(
                weights.astype(jnp.bfloat16), tab_v[h, seen, :], preferred_element_type=jnp.float32
            )
            return mixed, total

        if span == chunk:
            mixed, total = part(0)
        else:
            def step(c, carry):
                mixed, total = part(c)
                return carry[0] + mixed, carry[1] + total
            mixed, total = lax.fori_loop(
                0, span // chunk, step,
                (jnp.zeros((group * block, HD), jnp.float32), jnp.zeros((group * block, 1), jnp.float32)),
            )
        result = (mixed / total).astype(jnp.bfloat16)
        for g in range(group):
            obuf[h, here, g * HD:(g + 1) * HD] = result[g * block:(g + 1) * block]

    def outgoing(h, i):
        return pltpu.make_async_remote_copy(
            src_ref=obuf.at[h, pl.ds(pl.multiple_of(u_peer(i) * local, local), local), :],
            dst_ref=out_ref.at[:, pl.ds(pl.multiple_of((me * kvl + h) * qw, qw), qw)],
            send_sem=o_send.at[h, i - 1], recv_sem=o_recv.at[h, i - 1],
            device_id={"ulysses": u_peer(i)}, device_id_type=MESH,
        )

    def own_out(h):
        return pltpu.make_async_copy(
            obuf.at[h, pl.ds(pl.multiple_of(me * local, local), local), :],
            out_ref.at[:, pl.ds(pl.multiple_of((me * kvl + h) * qw, qw), qw)],
            o_local.at[h],
        )

    for h in range(kvl):
        for hop in range(1, back + 1):
            @pl.when(blk >= hop)
            def _():
                onward(0, h, hop).wait_recv()
                onward(1, h, hop).wait_recv()
        arrive(2, h)
        if rows // block <= 4:
            for i in range(rows // block):
                attend(h, i)
        else:
            def each(i, carry):
                attend(h, i)
                return carry
            lax.fori_loop(0, rows // block, each, 0)
        for i in range(1, ulysses):
            outgoing(h, i).start()
        own_out(h).start()

    own_page(0).wait()
    own_page(1).wait()
    for i in range(1, sources):
        handed(0, i).wait_recv()
        handed(1, i).wait_recv()
    for j in range(slots):
        def step(n, found, j=j):
            s = n // slots
            page = table_ref[lax.rem(s, cores), (s // cores) * slots + lax.rem(n, slots)]
            return found + jnp.where(page == mine * slots + j, s, 0)
        source = lax.fori_loop(0, sources * slots, step, jnp.int32(0))
        ck_ref[j] = pick(source, [got_k[s] for s in range(sources)])
        cv_ref[j] = pick(source, [got_v[s] for s in range(sources)])

    for i in range(1, sources):
        handed(0, i).wait_send()
        handed(1, i).wait_send()
    for what, h in order:
        for i in range(1, ulysses):
            incoming(what, h, i).wait_send()
    for h in range(kvl):
        for hop in range(1, back + 1):
            @pl.when(blk + hop < blks)
            def _():
                onward(0, h, hop).wait_send()
                onward(1, h, hop).wait_send()
    for h in range(kvl):
        own_out(h).wait()
        for i in range(1, ulysses):
            outgoing(h, i).wait()


def paired(
    sizes, q_ref, k_ref, v_ref, freq_ref, pages_ref, table_ref,
    out_ref, ck_ref, cv_ref,
    qraw, kraw, qrot, krot, tab_k, tab_v, qbuf, obuf, out_k, out_v, got_k, got_v,
    load_sem, kv_send, kv_recv, v_local, q_send, q_recv, x_send, x_recv, c_send, c_recv, c_local, o_send, o_recv,
):
    ulysses, blks, cores, kvl, group, halo, reqs, per = sizes
    rows = ulysses * PAGE
    sources = blks * cores
    home = halo * PAGE
    picks = ulysses // 2
    steps = picks * kvl // per
    inner = kvl // per
    kw = per * HD
    qw = per * group * HD
    me = lax.axis_index("ulysses")
    blk = lax.axis_index("blk")
    pack = lax.axis_index("handoff")
    mine = blk * cores + pack
    side = lax.rem(me, 2)
    duo = lax.div(me, 2)
    mate = me + 1 - 2 * side

    loads = [
        pltpu.make_async_copy(k_ref, kraw, load_sem.at[0]),
        pltpu.make_async_copy(q_ref, qraw, load_sem.at[1]),
    ]
    for load in loads:
        load.start()

    barrier = pltpu.get_barrier_semaphore()

    def u_peer(i):
        return lax.rem(me + i, ulysses)

    def u_source(i):
        return lax.rem(me + ulysses - i, ulysses)

    def s_peer(i):
        p = lax.rem(mine + i, sources)
        return p, {"blk": p // cores, "handoff": lax.rem(p, cores)}

    for i in range(1, ulysses):
        pl.semaphore_signal(barrier, inc=1, device_id={"ulysses": u_peer(i)}, device_id_type=MESH)
    for i in range(1, sources):
        pl.semaphore_signal(barrier, inc=1, device_id=s_peer(i)[1], device_id_type=MESH)

    def columns(whose, t, width):
        chosen = lax.rem(whose + 2 * (t // inner), ulysses)
        return pl.ds(pl.multiple_of((chosen * inner + t % inner) * width, width), width)

    def page_rows(page):
        return pl.ds(pl.multiple_of(home + page * PAGE, PAGE), PAGE)

    own_rows = pl.ds(pl.multiple_of(side * PAGE, PAGE), PAGE)
    mate_rows = pl.ds(pl.multiple_of((1 - side) * PAGE, PAGE), PAGE)

    def own_values(t):
        return pltpu.make_async_copy(
            v_ref.at[:, columns(me, t, kw)], tab_v.at[page_rows(me), t * kw:(t + 1) * kw], v_local.at[t]
        )

    for t in range(steps):
        own_values(t).start()

    @pl.when(blk == 0)
    def _():
        tab_k[0:home, :] = jnp.zeros((home, steps * kw), jnp.bfloat16)
        tab_v[0:home, :] = jnp.zeros((home, steps * kw), jnp.bfloat16)

    starts = []
    total = jnp.int32(0)
    for r in range(reqs):
        starts.append(total)
        total = total + pages_ref[pack, r] * PAGE

    def first_token(pos):
        first = jnp.zeros_like(pos)
        for r in range(reqs):
            first = jnp.maximum(first, jnp.where(pos >= starts[r], starts[r], 0))
        return first

    pos = blk * rows + me * PAGE + lax.broadcasted_iota(jnp.int32, (PAGE, HD), 0)
    angles = (pos - first_token(pos)).astype(jnp.float32) * freq_ref[...]
    lanes = lax.broadcasted_iota(jnp.int32, (PAGE, HD), 1)
    cosine = jnp.cos(angles)
    sine = jnp.sin(angles)
    sine = jnp.where(lanes < HD // 2, -sine, sine)

    loads[0].wait()
    for h in range(KVH):
        at = slice(h * HD, (h + 1) * HD)
        krot[:, at] = turn(kraw[:, at], cosine, sine)
    loads[1].wait()
    for h in range(KVH * group):
        at = slice(h * HD, (h + 1) * HD)
        qrot[:, at] = turn(qraw[:, at], cosine, sine)

    pl.semaphore_wait(barrier, ulysses - 1 + sources - 1)

    def needed(page, reader, t):
        if t < inner:
            return None
        lower = page <= 2 * lax.div(reader, 2) + 1
        return lower | (blk + 1 < blks)

    def guarded(condition, action):
        if condition is None:
            action()
        else:
            pl.when(condition)(action)

    def spread(which, t, i):
        src = (krot, v_ref)[which]
        tab = (tab_k, tab_v)[which]
        return pltpu.make_async_remote_copy(
            src_ref=src.at[:, columns(u_peer(i), t, kw)],
            dst_ref=tab.at[page_rows(me), t * kw:(t + 1) * kw],
            send_sem=kv_send.at[which, t, i - 1], recv_sem=kv_recv.at[which, t, i - 1],
            device_id={"ulysses": u_peer(i)}, device_id_type=MESH,
        )

    def asked(t):
        return pltpu.make_async_remote_copy(
            src_ref=qrot.at[:, columns(mate, t, qw)],
            dst_ref=qbuf.at[own_rows, t * qw:(t + 1) * qw],
            send_sem=q_send.at[t], recv_sem=q_recv.at[t],
            device_id={"ulysses": mate}, device_id_type=MESH,
        )

    for t in range(steps):
        for i in range(1, ulysses):
            def go(i=i, t=t):
                spread(0, t, i).start()
                spread(1, t, i).start()
            guarded(needed(me, u_peer(i), t), go)
        asked(t).start()

    for t in range(steps):
        tab_k[page_rows(me), t * kw:(t + 1) * kw] = krot[:, columns(me, t, kw)]
        qbuf[own_rows, t * qw:(t + 1) * qw] = qrot[:, columns(me, t, qw)]

    def onward(which, t, low):
        tab = (tab_k, tab_v)[which]
        count = (halo - low) * PAGE
        return pltpu.make_async_remote_copy(
            src_ref=tab.at[home + rows - count:home + rows, t * kw:(t + 1) * kw],
            dst_ref=tab.at[low * PAGE:halo * PAGE, t * kw:(t + 1) * kw],
            send_sem=x_send.at[which, t], recv_sem=x_recv.at[which, t],
            device_id={"blk": lax.rem(blk + 1, blks)}, device_id_type=MESH,
        )

    def each_halo(condition, action):
        for d in range(ulysses // 2):
            if 2 * d < halo:
                pl.when(condition & (duo == d))(functools.partial(action, 2 * d))

    def page_for(owner):
        def step(j, found):
            page = table_ref[pack, blk * ulysses + j]
            return found + jnp.where(lax.div(page, jnp.int32(ulysses)) == owner, j, 0)
        return lax.fori_loop(0, ulysses, step, jnp.int32(0))

    def handed(which, i):
        src, dst = ((out_k, got_k), (out_v, got_v))[which]
        return pltpu.make_async_remote_copy(
            src_ref=src.at[i], dst_ref=dst.at[mine],
            send_sem=c_send.at[which, i - 1], recv_sem=c_recv.at[which, i - 1],
            device_id=s_peer(i)[1], device_id_type=MESH,
        )

    def own_page(which):
        src, dst = ((out_k, got_k), (out_v, got_v))[which]
        return pltpu.make_async_copy(src.at[0], dst.at[mine], c_local.at[which])

    def hand_over():
        for i in range(sources):
            chosen = page_for(s_peer(i)[0])
            for tab, out in ((tab_k, out_k), (tab_v, out_v)):
                for h in range(kvl):
                    out[i, h] = pick(chosen, [
                        tab[home + j * PAGE:home + (j + 1) * PAGE, h * HD:(h + 1) * HD] for j in range(ulysses)
                    ])
        for i in range(1, sources):
            handed(0, i).start()
            handed(1, i).start()
        own_page(0).start()
        own_page(1).start()

    block = 2 * PAGE
    span = home + block
    factor = QUERY_SCALE / SOFT_CAP
    begin = pl.multiple_of(duo * block, block)
    seen = pl.ds(begin, span)
    q_pos = blk * rows + duo * block + lax.broadcasted_iota(jnp.int32, (block, 1), 0)
    q_low = jnp.maximum(first_token(q_pos), q_pos - (WINDOW - 1))
    key_pos = blk * rows - home + begin + lax.broadcasted_iota(jnp.int32, (1, span), 1)
    allowed = (key_pos <= q_pos) & (key_pos >= q_low)
    allowed = jnp.concatenate([allowed] * group, axis=0)

    def attend(h):
        query = jnp.concatenate(
            [qbuf[:, (h * group + g) * HD:(h * group + g + 1) * HD] for g in range(group)], axis=0
        )
        scores = lax.dot_general(
            query, tab_k[seen, h * HD:(h + 1) * HD], (((1,), (1,)), ((), ())), preferred_element_type=jnp.float32
        )
        weights = jnp.exp(SOFT_CAP * jnp.tanh(scores * factor))
        weights = jnp.where(allowed, weights, 0.0)
        total = jnp.sum(weights, axis=1, keepdims=True)
        mixed = jnp.dot(
            weights.astype(jnp.bfloat16), tab_v[seen, h * HD:(h + 1) * HD], preferred_element_type=jnp.float32
        )
        result = (mixed / total).astype(jnp.bfloat16)
        for g in range(group):
            obuf[:, (h * group + g) * HD:(h * group + g + 1) * HD] = result[g * block:(g + 1) * block]

    def outgoing(t):
        return pltpu.make_async_remote_copy(
            src_ref=obuf.at[mate_rows, t * qw:(t + 1) * qw],
            dst_ref=out_ref.at[:, columns(me, t, qw)],
            send_sem=o_send.at[t], recv_sem=o_recv.at[t],
            device_id={"ulysses": mate}, device_id_type=MESH,
        )

    def relay(t):
        own_values(t).wait()
        for i in range(1, ulysses):
            def landed(i=i):
                spread(0, t, i).wait_recv()
                spread(1, t, i).wait_recv()
            guarded(needed(u_source(i), me, t), landed)

        def send_on(low):
            onward(0, t, low).start()
            onward(1, t, low).start()

        each_halo(blk + 1 < blks, send_on)
        if t == inner - 1:
            hand_over()

    def work(t):
        def receive(low):
            onward(0, t, low).wait_recv()
            onward(1, t, low).wait_recv()

        each_halo(blk > 0, receive)
        asked(t).wait_recv()
        for h in range(t * per, (t + 1) * per):
            attend(h)
        outgoing(t).start()
        out_ref[:, columns(me, t, qw)] = obuf[own_rows, t * qw:(t + 1) * qw]

    for t in range(steps + LAG):
        if t < steps:
            relay(t)
        if t >= LAG:
            work(t - LAG)

    own_page(0).wait()
    own_page(1).wait()
    for i in range(1, sources):
        handed(0, i).wait_recv()
        handed(1, i).wait_recv()
    for j in range(ulysses):
        def step(n, found, j=j):
            s = n // ulysses
            page = table_ref[lax.rem(s, cores), (s // cores) * ulysses + lax.rem(n, ulysses)]
            return found + jnp.where(page == mine * ulysses + j, s, 0)
        source = lax.fori_loop(0, sources * ulysses, step, jnp.int32(0))
        ck_ref[j] = pick(source, [got_k[s] for s in range(sources)])
        cv_ref[j] = pick(source, [got_v[s] for s in range(sources)])

    for i in range(1, sources):
        handed(0, i).wait_send()
        handed(1, i).wait_send()
    for t in range(steps):
        for i in range(1, ulysses):
            def sent(i=i, t=t):
                spread(0, t, i).wait_send()
                spread(1, t, i).wait_send()
            guarded(needed(me, u_peer(i), t), sent)
        asked(t).wait_send()

        def passed(low, t=t):
            onward(0, t, low).wait_send()
            onward(1, t, low).wait_send()

        each_halo(blk + 1 < blks, passed)
        outgoing(t).wait()


def place(*refs):
    count = (len(refs) - 1) // 2
    sem = refs[-1]
    copies = [pltpu.make_async_copy(refs[i], refs[count + i], sem.at[i]) for i in range(count)]
    for copy in copies:
        copy.start()
    for copy in copies:
        copy.wait()


def body(queries, keys, values, request_pages, page_table):
    local = queries.shape[1]
    ulysses = lax.axis_size("ulysses")
    blks = lax.axis_size("blk")
    cores = lax.axis_size("handoff")
    kvl = KVH // ulysses
    group = QH // KVH
    rows = local * ulysses
    slots = rows // PAGE
    sources = blks * cores
    assert slots == sources
    reach = min(WINDOW, page_table.shape[1] // 2 * PAGE)
    back = min(-(-reach // rows), blks - 1)
    reqs = request_pages.shape[1]
    half = np.arange(HD // 2, dtype=np.float64)
    freq = (ROPE_BASE ** (-2.0 * half / HD)).astype(np.float32)
    freq = jnp.asarray(np.concatenate([freq, freq])[None, :])
    sizes = (ulysses, blks, cores, local, kvl, group, reach, reqs)
    qw = group * HD
    halo = reach // PAGE - 1
    per = min(1, kvl)
    bf = jnp.bfloat16
    dma = pltpu.SemaphoreType.DMA
    hops = max(back, 1)
    anywhere = pl.BlockSpec(memory_space=pl.ANY)
    vmem = pl.BlockSpec(memory_space=pltpu.VMEM)
    smem = pl.BlockSpec(memory_space=pltpu.SMEM)
    narrow = local == PAGE and ulysses % 2 == 0 and 0 < halo <= ulysses and kvl % per == 0 and blks > 1
    if narrow:
        held = ulysses // 2 * kvl
        steps = held // per
        run = functools.partial(paired, (ulysses, blks, cores, kvl, group, halo, reqs, per))
        table = pltpu.VMEM((halo * PAGE + rows, held * HD), bf)
        handing = pltpu.VMEM((sources, kvl, PAGE, HD), bf)
        scratch = [
            pltpu.VMEM((PAGE, QH * HD), bf),
            pltpu.VMEM((PAGE, KVH * HD), bf),
            pltpu.VMEM((PAGE, QH * HD), bf),
            pltpu.VMEM((PAGE, KVH * HD), bf),
            table, table,
            pltpu.VMEM((2 * PAGE, held * qw), bf),
            pltpu.VMEM((2 * PAGE, held * qw), bf),
            handing, handing, handing, handing,
            dma((2,)),
            dma((2, steps, ulysses - 1)),
            dma((2, steps, ulysses - 1)),
            dma((steps,)),
            dma((steps,)),
            dma((steps,)),
            dma((2, steps)),
            dma((2, steps)),
            dma((2, sources - 1)),
            dma((2, sources - 1)),
            dma((2,)),
            dma((steps,)),
            dma((steps,)),
        ]
    else:
        run = functools.partial(kernel, sizes)
        scratch = [
            pltpu.VMEM((kvl, rows, HD), bf),
            pltpu.VMEM((kvl, (back + 1) * rows, HD), bf),
            pltpu.VMEM((kvl, (back + 1) * rows, HD), bf),
            pltpu.VMEM((kvl, rows, qw), bf),
            pltpu.VMEM((kvl, rows, qw), bf),
            pltpu.VMEM((rows, HD), jnp.float32),
            pltpu.VMEM((rows, HD), jnp.float32),
            pltpu.VMEM((sources, kvl, PAGE, HD), bf),
            pltpu.VMEM((sources, kvl, PAGE, HD), bf),
            pltpu.VMEM((sources, kvl, PAGE, HD), bf),
            pltpu.VMEM((sources, kvl, PAGE, HD), bf),
            dma((3, kvl, ulysses - 1)),
            dma((3, kvl, ulysses - 1)),
            dma((3, kvl)),
            dma((2, kvl, hops)),
            dma((2, kvl, hops)),
            dma((2, sources - 1)),
            dma((2, sources - 1)),
            dma((2,)),
            dma((kvl, ulysses - 1)),
            dma((kvl, ulysses - 1)),
            dma((kvl,)),
        ]
    results = pl.pallas_call(
        run,
        out_shape=(
            pltpu.VMEM((local, QH * HD), bf),
            pltpu.VMEM((slots, kvl, PAGE, HD), bf),
            pltpu.VMEM((slots, kvl, PAGE, HD), bf),
        ),
        in_specs=[anywhere, anywhere, anywhere, vmem, smem, smem],
        out_specs=(vmem, vmem, vmem),
        scratch_shapes=scratch,
        compiler_params=pltpu.CompilerParams(collective_id=0, has_side_effects=True),
    )(queries[0], keys[0], values[0], freq, request_pages, page_table)
    results = [pltpu.with_memory_space_constraint(x, pltpu.VMEM) for x in results]
    attended, cache_keys, cache_values = pl.pallas_call(
        place,
        out_shape=tuple(jax.ShapeDtypeStruct(x.shape, x.dtype) for x in results),
        in_specs=[anywhere] * len(results),
        out_specs=(anywhere,) * len(results),
        scratch_shapes=[dma((len(results),))],
        compiler_params=pltpu.CompilerParams(vmem_limit_bytes=1 << 20),
    )(*results)
    return (attended[None], cache_keys, cache_values)


def solution(mesh):
    in_specs = (
        P(("groups", "handoff"), ("blk", "ulysses"), None),
        P(("groups", "handoff"), ("blk", "ulysses"), None),
        P(("groups", "handoff"), ("blk", "ulysses"), None),
        P("groups", None),
        P("groups", None),
    )
    out_specs = (
        P(("groups", "handoff"), ("blk", "ulysses"), None),
        P(("groups", "blk", "handoff"), "ulysses", None, None),
        P(("groups", "blk", "handoff"), "ulysses", None, None),
    )
    return jax.shard_map(body, mesh=mesh, in_specs=in_specs, out_specs=out_specs, check_vma=False)
```

```python
import functools

import jax
import jax.numpy as jnp
import numpy as np
from jax import lax
from jax.experimental import pallas as pl
from jax.experimental.pallas import tpu as pltpu
from jax.sharding import PartitionSpec as P

QH = 32
KVH = 16
HD = 128
WINDOW = 4096
PAGE = 64

QUERY_SCALE = 144.0 ** (-0.5)
SOFT_CAP = 50.0
ROPE_BASE = 10000.0
MESH = pl.DeviceIdType.MESH
LAG = 3


def turn(x, cosine, sine):
    wide = x.astype(jnp.float32)
    return (wide * cosine + pltpu.roll(wide, HD // 2, 1) * sine).astype(jnp.bfloat16)


def pick(index, choices):
    chosen = choices[0]
    for j in range(1, len(choices)):
        chosen = jnp.where(index == j, choices[j], chosen)
    return chosen


def kernel(
    sizes, q_ref, k_ref, v_ref, freq_ref, pages_ref, table_ref,
    out_ref, ck_ref, cv_ref,
    kraw, tab_k, tab_v, qbuf, obuf, cos_t, sin_t, out_k, out_v, got_k, got_v,
    in_send, in_recv, in_local, x_send, x_recv, c_send, c_recv, c_local, o_send, o_recv, o_local,
):
    ulysses, blks, cores, local, kvl, group, reach, reqs = sizes
    rows = ulysses * local
    slots = rows // PAGE
    sources = blks * cores
    back = min(-(-reach // rows), blks - 1)
    home = back * rows
    qw = group * HD
    me = lax.axis_index("ulysses")
    blk = lax.axis_index("blk")
    pack = lax.axis_index("handoff")
    mine = blk * cores + pack

    barrier = pltpu.get_barrier_semaphore()

    def u_peer(i):
        return lax.rem(me + i, ulysses)

    def s_peer(i):
        p = lax.rem(mine + i, sources)
        return p, {"blk": p // cores, "handoff": lax.rem(p, cores)}

    for i in range(1, ulysses):
        pl.semaphore_signal(barrier, inc=1, device_id={"ulysses": u_peer(i)}, device_id_type=MESH)
    for i in range(1, sources):
        pl.semaphore_signal(barrier, inc=1, device_id=s_peer(i)[1], device_id_type=MESH)

    for hop in range(1, back + 1):
        @pl.when(blk < hop)
        def _():
            part = pl.ds((back - hop) * rows, rows)
            tab_k[:, part, :] = jnp.zeros((kvl, rows, HD), jnp.bfloat16)
            tab_v[:, part, :] = jnp.zeros((kvl, rows, HD), jnp.bfloat16)

    pl.semaphore_wait(barrier, ulysses - 1 + sources - 1)

    def landing(what, h, whose):
        if what == 0:
            return kraw.at[h, pl.ds(whose * local, local), :]
        if what == 1:
            return tab_v.at[h, pl.ds(home + whose * local, local), :]
        return qbuf.at[h, pl.ds(whose * local, local), :]

    def leaving(what, h, whose):
        width = qw if what == 2 else HD
        ref = (k_ref, v_ref, q_ref)[what]
        return ref.at[:, pl.ds(pl.multiple_of((whose * kvl + h) * width, width), width)]

    def incoming(what, h, i):
        return pltpu.make_async_remote_copy(
            src_ref=leaving(what, h, u_peer(i)), dst_ref=landing(what, h, me),
            send_sem=in_send.at[what, h, i - 1], recv_sem=in_recv.at[what, h, i - 1],
            device_id={"ulysses": u_peer(i)}, device_id_type=MESH,
        )

    def own_in(what, h):
        return pltpu.make_async_copy(leaving(what, h, me), landing(what, h, me), in_local.at[what, h])

    order = [(w, h) for h in range(kvl) for w in (0, 1)] + [(2, h) for h in range(kvl)]
    for what, h in order:
        for i in range(1, ulysses):
            incoming(what, h, i).start()
        own_in(what, h).start()

    def arrive(what, h):
        own_in(what, h).wait()
        for i in range(1, ulysses):
            incoming(what, h, i).wait_recv()

    ends = []
    starts = []
    total = jnp.int32(0)
    for r in range(reqs):
        starts.append(total)
        total = total + pages_ref[pack, r] * PAGE
        ends.append(total)

    def first_token(pos):
        first = jnp.zeros_like(pos)
        for r in range(reqs):
            first = jnp.maximum(first, jnp.where(pos >= starts[r], starts[r], 0))
        return first

    pos_rows = blk * rows + lax.broadcasted_iota(jnp.int32, (rows, HD), 0)
    rel = (pos_rows - first_token(pos_rows)).astype(jnp.float32)
    angles = rel * freq_ref[...]
    lanes = lax.broadcasted_iota(jnp.int32, (rows, HD), 1)
    cos_t[...] = jnp.cos(angles)
    sine = jnp.sin(angles)
    sin_t[...] = jnp.where(lanes < HD // 2, -sine, sine)

    def onward(which, h, hop):
        tab = (tab_k, tab_v)[which]
        return pltpu.make_async_remote_copy(
            src_ref=tab.at[h, pl.ds(home, rows), :],
            dst_ref=tab.at[h, pl.ds((back - hop) * rows, rows), :],
            send_sem=x_send.at[which, h, hop - 1], recv_sem=x_recv.at[which, h, hop - 1],
            device_id={"blk": lax.rem(blk + hop, blks)}, device_id_type=MESH,
        )

    for h in range(kvl):
        arrive(0, h)
        tab_k[h, pl.ds(home, rows), :] = turn(kraw[h], cos_t[...], sin_t[...])
        arrive(1, h)
        for hop in range(1, back + 1):
            @pl.when(blk + hop < blks)
            def _():
                onward(0, h, hop).start()
                onward(1, h, hop).start()

    def page_for(owner):
        def step(j, found):
            page = table_ref[pack, blk * slots + j]
            return found + jnp.where(lax.div(page, jnp.int32(slots)) == owner, j, 0)
        return lax.fori_loop(0, slots, step, jnp.int32(0))

    def handed(which, i):
        src, dst = ((out_k, got_k), (out_v, got_v))[which]
        return pltpu.make_async_remote_copy(
            src_ref=src.at[i], dst_ref=dst.at[mine],
            send_sem=c_send.at[which, i - 1], recv_sem=c_recv.at[which, i - 1],
            device_id=s_peer(i)[1], device_id_type=MESH,
        )

    def own_page(which):
        src, dst = ((out_k, got_k), (out_v, got_v))[which]
        return pltpu.make_async_copy(src.at[0], dst.at[mine], c_local.at[which])

    for i in range(sources):
        chosen = page_for(s_peer(i)[0])
        for tab, out in ((tab_k, out_k), (tab_v, out_v)):
            out[i] = pick(chosen, [tab[:, home + j * PAGE:home + (j + 1) * PAGE, :] for j in range(slots)])
    for i in range(1, sources):
        handed(0, i).start()
        handed(1, i).start()
    own_page(0).start()
    own_page(1).start()

    block = min(rows, 128)
    lead = min(-(-reach // block) * block, home)
    span = lead + block
    chunk = span if span <= 512 else block
    factor = QUERY_SCALE / SOFT_CAP

    def attend(h, i):
        at = i * block
        if not isinstance(i, int):
            at = pl.multiple_of(at, block)
        here = pl.ds(at, block)
        cosine, sine_here = cos_t[here, :], sin_t[here, :]
        query = jnp.concatenate(
            [turn(qbuf[h, here, g * HD:(g + 1) * HD], cosine, sine_here) for g in range(group)], axis=0
        )
        pos = blk * rows + at + lax.broadcasted_iota(jnp.int32, (block, 1), 0)
        low = jnp.maximum(first_token(pos), pos - (WINDOW - 1))
        pos = jnp.concatenate([pos] * group, axis=0)
        low = jnp.concatenate([low] * group, axis=0)
        begin = home + at - lead

        def part(c):
            start = begin + c * chunk
            if not isinstance(start, int):
                start = pl.multiple_of(start, block)
            seen = pl.ds(start, chunk)
            scores = lax.dot_general(
                query, tab_k[h, seen, :], (((1,), (1,)), ((), ())), preferred_element_type=jnp.float32
            )
            weights = jnp.exp(SOFT_CAP * jnp.tanh(scores * factor))
            key_pos = (blk - back) * rows + start + lax.broadcasted_iota(jnp.int32, (1, chunk), 1)
            weights = jnp.where((key_pos <= pos) & (key_pos >= low), weights, 0.0)
            total = jnp.sum(weights, axis=1, keepdims=True)
            mixed = jnp.dot(
                weights.astype(jnp.bfloat16), tab_v[h, seen, :], preferred_element_type=jnp.float32
            )
            return mixed, total

        if span == chunk:
            mixed, total = part(0)
        else:
            def step(c, carry):
                mixed, total = part(c)
                return carry[0] + mixed, carry[1] + total
            mixed, total = lax.fori_loop(
                0, span // chunk, step,
                (jnp.zeros((group * block, HD), jnp.float32), jnp.zeros((group * block, 1), jnp.float32)),
            )
        result = (mixed / total).astype(jnp.bfloat16)
        for g in range(group):
            obuf[h, here, g * HD:(g + 1) * HD] = result[g * block:(g + 1) * block]

    def outgoing(h, i):
        return pltpu.make_async_remote_copy(
            src_ref=obuf.at[h, pl.ds(pl.multiple_of(u_peer(i) * local, local), local), :],
            dst_ref=out_ref.at[:, pl.ds(pl.multiple_of((me * kvl + h) * qw, qw), qw)],
            send_sem=o_send.at[h, i - 1], recv_sem=o_recv.at[h, i - 1],
            device_id={"ulysses": u_peer(i)}, device_id_type=MESH,
        )

    def own_out(h):
        return pltpu.make_async_copy(
            obuf.at[h, pl.ds(pl.multiple_of(me * local, local), local), :],
            out_ref.at[:, pl.ds(pl.multiple_of((me * kvl + h) * qw, qw), qw)],
            o_local.at[h],
        )

    for h in range(kvl):
        for hop in range(1, back + 1):
            @pl.when(blk >= hop)
            def _():
                onward(0, h, hop).wait_recv()
                onward(1, h, hop).wait_recv()
        arrive(2, h)
        if rows // block <= 4:
            for i in range(rows // block):
                attend(h, i)
        else:
            def each(i, carry):
                attend(h, i)
                return carry
            lax.fori_loop(0, rows // block, each, 0)
        for i in range(1, ulysses):
            outgoing(h, i).start()
        own_out(h).start()

    own_page(0).wait()
    own_page(1).wait()
    for i in range(1, sources):
        handed(0, i).wait_recv()
        handed(1, i).wait_recv()
    for j in range(slots):
        def step(n, found, j=j):
            s = n // slots
            page = table_ref[lax.rem(s, cores), (s // cores) * slots + lax.rem(n, slots)]
            return found + jnp.where(page == mine * slots + j, s, 0)
        source = lax.fori_loop(0, sources * slots, step, jnp.int32(0))
        ck_ref[j] = pick(source, [got_k[s] for s in range(sources)])
        cv_ref[j] = pick(source, [got_v[s] for s in range(sources)])

    for i in range(1, sources):
        handed(0, i).wait_send()
        handed(1, i).wait_send()
    for what, h in order:
        for i in range(1, ulysses):
            incoming(what, h, i).wait_send()
    for h in range(kvl):
        for hop in range(1, back + 1):
            @pl.when(blk + hop < blks)
            def _():
                onward(0, h, hop).wait_send()
                onward(1, h, hop).wait_send()
    for h in range(kvl):
        own_out(h).wait()
        for i in range(1, ulysses):
            outgoing(h, i).wait()


def paired(
    sizes, q_ref, k_ref, v_ref, freq_ref, pages_ref, table_ref,
    out_ref, ck_ref, cv_ref,
    qraw, kraw, qrot, krot, tab_k, tab_v, qbuf, obuf, out_k, out_v, got_k, got_v,
    load_sem, kv_send, kv_recv, v_local, q_send, q_recv, x_send, x_recv, c_send, c_recv, c_local, o_send, o_recv,
):
    ulysses, blks, cores, kvl, group, halo, reqs, per = sizes
    rows = ulysses * PAGE
    sources = blks * cores
    home = halo * PAGE
    picks = ulysses // 2
    steps = picks * kvl // per
    inner = kvl // per
    kw = per * HD
    qw = per * group * HD
    me = lax.axis_index("ulysses")
    blk = lax.axis_index("blk")
    pack = lax.axis_index("handoff")
    mine = blk * cores + pack
    side = lax.rem(me, 2)
    duo = lax.div(me, 2)
    mate = me + 1 - 2 * side

    loads = [
        pltpu.make_async_copy(k_ref, kraw, load_sem.at[0]),
        pltpu.make_async_copy(q_ref, qraw, load_sem.at[1]),
    ]
    for load in loads:
        load.start()

    barrier = pltpu.get_barrier_semaphore()

    def u_peer(i):
        return lax.rem(me + i, ulysses)

    def u_source(i):
        return lax.rem(me + ulysses - i, ulysses)

    def s_peer(i):
        p = lax.rem(mine + i, sources)
        return p, {"blk": p // cores, "handoff": lax.rem(p, cores)}

    for i in range(1, ulysses):
        pl.semaphore_signal(barrier, inc=1, device_id={"ulysses": u_peer(i)}, device_id_type=MESH)
    for i in range(1, sources):
        pl.semaphore_signal(barrier, inc=1, device_id=s_peer(i)[1], device_id_type=MESH)

    def columns(whose, t, width):
        chosen = lax.rem(whose + 2 * (t // inner), ulysses)
        return pl.ds(pl.multiple_of((chosen * inner + t % inner) * width, width), width)

    def page_rows(page):
        return pl.ds(pl.multiple_of(home + page * PAGE, PAGE), PAGE)

    own_rows = pl.ds(pl.multiple_of(side * PAGE, PAGE), PAGE)
    mate_rows = pl.ds(pl.multiple_of((1 - side) * PAGE, PAGE), PAGE)

    def own_values(t):
        return pltpu.make_async_copy(
            v_ref.at[:, columns(me, t, kw)], tab_v.at[page_rows(me), t * kw:(t + 1) * kw], v_local.at[t]
        )

    for t in range(steps):
        own_values(t).start()

    @pl.when(blk == 0)
    def _():
        tab_k[0:home, :] = jnp.zeros((home, steps * kw), jnp.bfloat16)
        tab_v[0:home, :] = jnp.zeros((home, steps * kw), jnp.bfloat16)

    starts = []
    total = jnp.int32(0)
    for r in range(reqs):
        starts.append(total)
        total = total + pages_ref[pack, r] * PAGE

    def first_token(pos):
        first = jnp.zeros_like(pos)
        for r in range(reqs):
            first = jnp.maximum(first, jnp.where(pos >= starts[r], starts[r], 0))
        return first

    pos = blk * rows + me * PAGE + lax.broadcasted_iota(jnp.int32, (PAGE, HD), 0)
    angles = (pos - first_token(pos)).astype(jnp.float32) * freq_ref[...]
    lanes = lax.broadcasted_iota(jnp.int32, (PAGE, HD), 1)
    cosine = jnp.cos(angles)
    sine = jnp.sin(angles)
    sine = jnp.where(lanes < HD // 2, -sine, sine)

    loads[0].wait()
    for h in range(KVH):
        at = slice(h * HD, (h + 1) * HD)
        krot[:, at] = turn(kraw[:, at], cosine, sine)
    loads[1].wait()
    for h in range(KVH * group):
        at = slice(h * HD, (h + 1) * HD)
        qrot[:, at] = turn(qraw[:, at], cosine, sine)

    pl.semaphore_wait(barrier, ulysses - 1 + sources - 1)

    def needed(page, reader, t):
        if t < inner:
            return None
        lower = page <= 2 * lax.div(reader, 2) + 1
        return lower | (blk + 1 < blks)

    def guarded(condition, action):
        if condition is None:
            action()
        else:
            pl.when(condition)(action)

    def spread(which, t, i):
        src = (krot, v_ref)[which]
        tab = (tab_k, tab_v)[which]
        return pltpu.make_async_remote_copy(
            src_ref=src.at[:, columns(u_peer(i), t, kw)],
            dst_ref=tab.at[page_rows(me), t * kw:(t + 1) * kw],
            send_sem=kv_send.at[which, t, i - 1], recv_sem=kv_recv.at[which, t, i - 1],
            device_id={"ulysses": u_peer(i)}, device_id_type=MESH,
        )

    def asked(t):
        return pltpu.make_async_remote_copy(
            src_ref=qrot.at[:, columns(mate, t, qw)],
            dst_ref=qbuf.at[own_rows, t * qw:(t + 1) * qw],
            send_sem=q_send.at[t], recv_sem=q_recv.at[t],
            device_id={"ulysses": mate}, device_id_type=MESH,
        )

    for t in range(steps):
        for i in range(1, ulysses):
            def go(i=i, t=t):
                spread(0, t, i).start()
                spread(1, t, i).start()
            guarded(needed(me, u_peer(i), t), go)
        asked(t).start()

    for t in range(steps):
        tab_k[page_rows(me), t * kw:(t + 1) * kw] = krot[:, columns(me, t, kw)]
        qbuf[own_rows, t * qw:(t + 1) * qw] = qrot[:, columns(me, t, qw)]

    def onward(which, t, low):
        tab = (tab_k, tab_v)[which]
        count = (halo - low) * PAGE
        return pltpu.make_async_remote_copy(
            src_ref=tab.at[home + rows - count:home + rows, t * kw:(t + 1) * kw],
            dst_ref=tab.at[low * PAGE:halo * PAGE, t * kw:(t + 1) * kw],
            send_sem=x_send.at[which, t], recv_sem=x_recv.at[which, t],
            device_id={"blk": lax.rem(blk + 1, blks)}, device_id_type=MESH,
        )

    def each_halo(condition, action):
        for d in range(ulysses // 2):
            if 2 * d < halo:
                pl.when(condition & (duo == d))(functools.partial(action, 2 * d))

    def page_for(owner):
        def step(j, found):
            page = table_ref[pack, blk * ulysses + j]
            return found + jnp.where(lax.div(page, jnp.int32(ulysses)) == owner, j, 0)
        return lax.fori_loop(0, ulysses, step, jnp.int32(0))

    def handed(which, i):
        src, dst = ((out_k, got_k), (out_v, got_v))[which]
        return pltpu.make_async_remote_copy(
            src_ref=src.at[i], dst_ref=dst.at[mine],
            send_sem=c_send.at[which, i - 1], recv_sem=c_recv.at[which, i - 1],
            device_id=s_peer(i)[1], device_id_type=MESH,
        )

    def own_page(which):
        src, dst = ((out_k, got_k), (out_v, got_v))[which]
        return pltpu.make_async_copy(src.at[0], dst.at[mine], c_local.at[which])

    def hand_over():
        for i in range(sources):
            chosen = page_for(s_peer(i)[0])
            for tab, out in ((tab_k, out_k), (tab_v, out_v)):
                for h in range(kvl):
                    out[i, h] = pick(chosen, [
                        tab[home + j * PAGE:home + (j + 1) * PAGE, h * HD:(h + 1) * HD] for j in range(ulysses)
                    ])
        for i in range(1, sources):
            handed(0, i).start()
            handed(1, i).start()
        own_page(0).start()
        own_page(1).start()

    block = 2 * PAGE
    span = home + block
    factor = QUERY_SCALE / SOFT_CAP
    begin = pl.multiple_of(duo * block, block)
    seen = pl.ds(begin, span)
    q_pos = blk * rows + duo * block + lax.broadcasted_iota(jnp.int32, (block, 1), 0)
    q_low = jnp.maximum(first_token(q_pos), q_pos - (WINDOW - 1))
    key_pos = blk * rows - home + begin + lax.broadcasted_iota(jnp.int32, (1, span), 1)
    allowed = (key_pos <= q_pos) & (key_pos >= q_low)
    allowed = jnp.concatenate([allowed] * group, axis=0)

    def attend(h):
        query = jnp.concatenate(
            [qbuf[:, (h * group + g) * HD:(h * group + g + 1) * HD] for g in range(group)], axis=0
        )
        scores = lax.dot_general(
            query, tab_k[seen, h * HD:(h + 1) * HD], (((1,), (1,)), ((), ())), preferred_element_type=jnp.float32
        )
        weights = jnp.exp(SOFT_CAP * jnp.tanh(scores * factor))
        weights = jnp.where(allowed, weights, 0.0)
        total = jnp.sum(weights, axis=1, keepdims=True)
        mixed = jnp.dot(
            weights.astype(jnp.bfloat16), tab_v[seen, h * HD:(h + 1) * HD], preferred_element_type=jnp.float32
        )
        result = (mixed / total).astype(jnp.bfloat16)
        for g in range(group):
            obuf[:, (h * group + g) * HD:(h * group + g + 1) * HD] = result[g * block:(g + 1) * block]

    def outgoing(t):
        return pltpu.make_async_remote_copy(
            src_ref=obuf.at[mate_rows, t * qw:(t + 1) * qw],
            dst_ref=out_ref.at[:, columns(me, t, qw)],
            send_sem=o_send.at[t], recv_sem=o_recv.at[t],
            device_id={"ulysses": mate}, device_id_type=MESH,
        )

    def relay(t):
        own_values(t).wait()
        for i in range(1, ulysses):
            def landed(i=i):
                spread(0, t, i).wait_recv()
                spread(1, t, i).wait_recv()
            guarded(needed(u_source(i), me, t), landed)

        def send_on(low):
            onward(0, t, low).start()
            onward(1, t, low).start()

        each_halo(blk + 1 < blks, send_on)
        if t == inner - 1:
            hand_over()

    def work(t):
        def receive(low):
            onward(0, t, low).wait_recv()
            onward(1, t, low).wait_recv()

        each_halo(blk > 0, receive)
        asked(t).wait_recv()
        for h in range(t * per, (t + 1) * per):
            attend(h)
        outgoing(t).start()
        out_ref[:, columns(me, t, qw)] = obuf[own_rows, t * qw:(t + 1) * qw]

    for t in range(steps + LAG):
        if t < steps:
            relay(t)
        if t >= LAG:
            work(t - LAG)

    own_page(0).wait()
    own_page(1).wait()
    for i in range(1, sources):
        handed(0, i).wait_recv()
        handed(1, i).wait_recv()
    for j in range(ulysses):
        def step(n, found, j=j):
            s = n // ulysses
            page = table_ref[lax.rem(s, cores), (s // cores) * ulysses + lax.rem(n, ulysses)]
            return found + jnp.where(page == mine * ulysses + j, s, 0)
        source = lax.fori_loop(0, sources * ulysses, step, jnp.int32(0))
        ck_ref[j] = pick(source, [got_k[s] for s in range(sources)])
        cv_ref[j] = pick(source, [got_v[s] for s in range(sources)])

    for i in range(1, sources):
        handed(0, i).wait_send()
        handed(1, i).wait_send()
    for t in range(steps):
        for i in range(1, ulysses):
            def sent(i=i, t=t):
                spread(0, t, i).wait_send()
                spread(1, t, i).wait_send()
            guarded(needed(me, u_peer(i), t), sent)
        asked(t).wait_send()

        def passed(low, t=t):
            onward(0, t, low).wait_send()
            onward(1, t, low).wait_send()

        each_halo(blk + 1 < blks, passed)
        outgoing(t).wait()


def place(*refs):
    count = (len(refs) - 1) // 2
    sem = refs[-1]
    copies = [pltpu.make_async_copy(refs[i], refs[count + i], sem.at[i]) for i in range(count)]
    for copy in copies:
        copy.start()
    for copy in copies:
        copy.wait()


def body(queries, keys, values, request_pages, page_table):
    local = queries.shape[1]
    ulysses = lax.axis_size("ulysses")
    blks = lax.axis_size("blk")
    cores = lax.axis_size("handoff")
    kvl = KVH // ulysses
    group = QH // KVH
    rows = local * ulysses
    slots = rows // PAGE
    sources = blks * cores
    assert slots == sources
    reach = min(WINDOW, page_table.shape[1] // 2 * PAGE)
    back = min(-(-reach // rows), blks - 1)
    reqs = request_pages.shape[1]
    half = np.arange(HD // 2, dtype=np.float64)
    freq = (ROPE_BASE ** (-2.0 * half / HD)).astype(np.float32)
    freq = jnp.asarray(np.concatenate([freq, freq])[None, :])
    sizes = (ulysses, blks, cores, local, kvl, group, reach, reqs)
    qw = group * HD
    halo = reach // PAGE - 1
    per = min(1, kvl)
    bf = jnp.bfloat16
    dma = pltpu.SemaphoreType.DMA
    hops = max(back, 1)
    anywhere = pl.BlockSpec(memory_space=pl.ANY)
    vmem = pl.BlockSpec(memory_space=pltpu.VMEM)
    smem = pl.BlockSpec(memory_space=pltpu.SMEM)
    narrow = local == PAGE and ulysses % 2 == 0 and 0 < halo <= ulysses and kvl % per == 0 and blks > 1
    if narrow:
        held = ulysses // 2 * kvl
        steps = held // per
        run = functools.partial(paired, (ulysses, blks, cores, kvl, group, halo, reqs, per))
        table = pltpu.VMEM((halo * PAGE + rows, held * HD), bf)
        handing = pltpu.VMEM((sources, kvl, PAGE, HD), bf)
        scratch = [
            pltpu.VMEM((PAGE, QH * HD), bf),
            pltpu.VMEM((PAGE, KVH * HD), bf),
            pltpu.VMEM((PAGE, QH * HD), bf),
            pltpu.VMEM((PAGE, KVH * HD), bf),
            table, table,
            pltpu.VMEM((2 * PAGE, held * qw), bf),
            pltpu.VMEM((2 * PAGE, held * qw), bf),
            handing, handing, handing, handing,
            dma((2,)),
            dma((2, steps, ulysses - 1)),
            dma((2, steps, ulysses - 1)),
            dma((steps,)),
            dma((steps,)),
            dma((steps,)),
            dma((2, steps)),
            dma((2, steps)),
            dma((2, sources - 1)),
            dma((2, sources - 1)),
            dma((2,)),
            dma((steps,)),
            dma((steps,)),
        ]
    else:
        run = functools.partial(kernel, sizes)
        scratch = [
            pltpu.VMEM((kvl, rows, HD), bf),
            pltpu.VMEM((kvl, (back + 1) * rows, HD), bf),
            pltpu.VMEM((kvl, (back + 1) * rows, HD), bf),
            pltpu.VMEM((kvl, rows, qw), bf),
            pltpu.VMEM((kvl, rows, qw), bf),
            pltpu.VMEM((rows, HD), jnp.float32),
            pltpu.VMEM((rows, HD), jnp.float32),
            pltpu.VMEM((sources, kvl, PAGE, HD), bf),
            pltpu.VMEM((sources, kvl, PAGE, HD), bf),
            pltpu.VMEM((sources, kvl, PAGE, HD), bf),
            pltpu.VMEM((sources, kvl, PAGE, HD), bf),
            dma((3, kvl, ulysses - 1)),
            dma((3, kvl, ulysses - 1)),
            dma((3, kvl)),
            dma((2, kvl, hops)),
            dma((2, kvl, hops)),
            dma((2, sources - 1)),
            dma((2, sources - 1)),
            dma((2,)),
            dma((kvl, ulysses - 1)),
            dma((kvl, ulysses - 1)),
            dma((kvl,)),
        ]
    results = pl.pallas_call(
        run,
        out_shape=(
            pltpu.VMEM((local, QH * HD), bf),
            pltpu.VMEM((slots, kvl, PAGE, HD), bf),
            pltpu.VMEM((slots, kvl, PAGE, HD), bf),
        ),
        in_specs=[anywhere, anywhere, anywhere, vmem, smem, smem],
        out_specs=(vmem, vmem, vmem),
        scratch_shapes=scratch,
        compiler_params=pltpu.CompilerParams(collective_id=0, has_side_effects=True),
    )(queries[0], keys[0], values[0], freq, request_pages, page_table)
    results = [pltpu.with_memory_space_constraint(x, pltpu.VMEM) for x in results]
    attended, cache_keys, cache_values = pl.pallas_call(
        place,
        out_shape=tuple(jax.ShapeDtypeStruct(x.shape, x.dtype) for x in results),
        in_specs=[anywhere] * len(results),
        out_specs=(anywhere,) * len(results),
        scratch_shapes=[dma((len(results),))],
        compiler_params=pltpu.CompilerParams(vmem_limit_bytes=1 << 20),
    )(*results)
    return (attended[None], cache_keys, cache_values)


def solution(mesh):
    in_specs = (
        P(("groups", "handoff"), ("blk", "ulysses"), None),
        P(("groups", "handoff"), ("blk", "ulysses"), None),
        P(("groups", "handoff"), ("blk", "ulysses"), None),
        P("groups", None),
        P("groups", None),
    )
    out_specs = (
        P(("groups", "handoff"), ("blk", "ulysses"), None),
        P(("groups", "blk", "handoff"), "ulysses", None, None),
        P(("groups", "blk", "handoff"), "ulysses", None, None),
    )
    return jax.shard_map(body, mesh=mesh, in_specs=in_specs, out_specs=out_specs, check_vma=False)
```
